256 devices in a mesh: group: 8 (over z), tok: 32 (over y, x, core).
Axes of the slice: x: 4, y: 4, z: 8, core: 2. Of those that a mesh axis runs over, the one named last changes fastest.
Arguments:
- query_rows: bfloat16 [8, 8192, 256], P('group', 'tok'), may hold values from -6 to 6
- key_rows: bfloat16 [8, 8192, 256], P('group', 'tok'), may hold values from -6 to 6
- value_rows: bfloat16 [8, 8192, 256], P('group', 'tok'), may hold values from -6 to 6
- token_rates: bfloat16 [8, 8192], P('group', 'tok'), may hold values from 0.099609375 to 1
- gate_init: float32 [256, 256], P('tok'), may hold values from -0.375 to 0.375
- up_init: float32 [256, 256], P('tok'), may hold values from -0.375 to 0.375
- down_init: float32 [256, 256], P('tok'), may hold values from -0.375 to 0.375
Outputs:
- outputs: bfloat16 [8, 8192, 256], P('group', 'tok')
- gate_out: float32 [8, 256, 256], P('group', 'tok')
- up_out: float32 [8, 256, 256], P('group', 'tok')
- down_out: float32 [8, 256, 256], P('group', 'tok')
The draws below stay inside these ranges and needn't reach their ends.
All inputs are finite; a program needn't handle non-finite values.
Results may differ from the reference program's by a relative error of at most 0.03.
Values may be sent and summed in bfloat16 or wider, within the bound.
A program may use at most 64 MiB of HBM per device.

```python
import math
import jax
import jax.numpy as jnp
from jax import lax

DH = 256
HID = 256
NS_STEPS = 3
GROUPS = 8
GROUP_TOK = 8192
N_GROUP = 8


def block_scale(stream_key, extent, split, least, high):
    gain = 1.0
    for dim, blocks in split:
        heights = jax.random.uniform(jax.random.fold_in(jax.random.fold_in(stream_key, 6), dim), (blocks,), jnp.float32, least / len(split), high / len(split))
        gain = gain * jnp.repeat(jnp.exp(heights), extent[dim] // blocks).reshape((-1,) + (1,) * (len(extent) - 1 - dim))
    return gain


def normal_values(key, shape, spread, most, cuts=(), dtype=jnp.bfloat16):
    loudness = block_scale(key, shape, cuts, -0.22, 0.18) if cuts else 1.0
    drawn = jax.random.normal(key, shape, jnp.float32) * spread * loudness
    return jnp.minimum(jnp.maximum(drawn, -most), most).astype(dtype)


def setup_inputs(seed: int = 0) -> dict:
    key_of = jax.random.split(jax.random.key(seed), 8)
    query_rows = normal_values(key_of[0], (GROUPS, GROUP_TOK, DH), 1.0, 6.0, ((0, 8), (1, 32)))
    key_rows = normal_values(key_of[1], (GROUPS, GROUP_TOK, DH), 1.0, 6.0, ((0, 8), (1, 32)))
    value_rows = normal_values(key_of[2], (GROUPS, GROUP_TOK, DH), 1.0, 6.0, ((0, 8), (1, 32)))
    token_rates = jnp.clip(jnp.exp(math.log(1.0) - 2.306499 * jax.random.uniform(key_of[3], (GROUPS, GROUP_TOK), jnp.float32) ** block_scale(key_of[3], (GROUPS, GROUP_TOK), ((0, 8), (1, 32)), -0.2, 0.2)), 0.099609375, 1.0).astype(jnp.bfloat16)
    gate_init = normal_values(key_of[4], (DH, HID), DH ** -0.5, 0.375, ((0, 32),), jnp.float32)
    up_init = normal_values(key_of[5], (DH, HID), DH ** -0.5, 0.375, ((0, 32),), jnp.float32)
    down_init = normal_values(key_of[6], (HID, DH), HID ** -0.5, 0.375, ((0, 32),), jnp.float32)
    return dict(query_rows=query_rows, key_rows=key_rows, value_rows=value_rows, token_rates=token_rates, gate_init=gate_init, up_init=up_init, down_init=down_init)


schulz_coeffs = (3.4445, -4.775, 2.0315)
update_scale = 0.5

def silu_parts(pre_values):
    sigmoid_val = jax.nn.sigmoid(pre_values)
    return (pre_values * sigmoid_val, sigmoid_val * (1.0 + pre_values * (1.0 - sigmoid_val)))

def orthogonalize(gradient):
    scaled = gradient * lax.rsqrt(jnp.sum(gradient * gradient) + 1e-06)
    for repeat in range(NS_STEPS):
        gram_full = jnp.dot(scaled, scaled.T, precision=lax.Precision.HIGHEST)
        square = jnp.dot(gram_full, gram_full, precision=lax.Precision.HIGHEST)
        poly_full = schulz_coeffs[1] * gram_full + schulz_coeffs[2] * square
        scaled = schulz_coeffs[0] * scaled + jnp.dot(poly_full, scaled, precision=lax.Precision.HIGHEST)
    return scaled

def renormalize(stepped, before):
    target = lax.optimization_barrier(jnp.sum(before * before, axis=0, keepdims=True))
    present = lax.optimization_barrier(jnp.sum(stepped * stepped, axis=0, keepdims=True))
    return stepped * jnp.sqrt(target) * lax.rsqrt(present + 1e-06)

def advance(weights, key_block, value_block, rate_block):
    gate_low, up_low, down_low = [w.astype(jnp.bfloat16) for w in weights]
    gate_pre = jnp.dot(key_block, gate_low, preferred_element_type=jnp.float32)
    up_pre = jnp.dot(key_block, up_low, preferred_element_type=jnp.float32)
    act_full, slope = silu_parts(gate_pre)
    act_low = (act_full * up_pre).astype(jnp.bfloat16)
    out_grad = (-(rate_block[:, None].astype(jnp.float32) * value_block.astype(jnp.float32))).astype(jnp.bfloat16)
    down_grad = jnp.dot(act_low.T, out_grad, preferred_element_type=jnp.float32)
    act_grad = jnp.dot(out_grad, down_low.T, preferred_element_type=jnp.float32)
    gate_diff = (act_grad * up_pre * slope).astype(jnp.bfloat16)
    up_diff = (act_grad * act_full).astype(jnp.bfloat16)
    gate_grad = jnp.dot(key_block.T, gate_diff, preferred_element_type=jnp.float32)
    up_grad = jnp.dot(key_block.T, up_diff, preferred_element_type=jnp.float32)
    grads = (gate_grad, up_grad, down_grad)
    return tuple((renormalize(w - update_scale * orthogonalize(g), w) for w, g in zip(weights, grads)))

def apply_fast(weights, query_block):
    gate_low, up_low, down_low = [w.astype(jnp.bfloat16) for w in weights]
    gate_pre = jnp.dot(query_block, gate_low, preferred_element_type=jnp.float32)
    up_pre = jnp.dot(query_block, up_low, preferred_element_type=jnp.float32)
    hidden = (jax.nn.silu(gate_pre) * up_pre).astype(jnp.bfloat16)
    return jnp.dot(hidden, down_low, preferred_element_type=jnp.float32).astype(jnp.bfloat16)

def reference(query_rows, key_rows, value_rows, token_rates, gate_init, up_init, down_init):
    current = (gate_init, up_init, down_init)
    results, gates, uppers, downs = ([], [], [], [])
    for block_idx in range(N_GROUP):
        results.append(apply_fast(current, query_rows[block_idx]))
        current = advance(current, key_rows[block_idx], value_rows[block_idx], token_rates[block_idx])
        gates.append(current[0])
        uppers.append(current[1])
        downs.append(current[2])
    return (jnp.stack(results), jnp.stack(gates), jnp.stack(uppers), jnp.stack(downs))
```

```python
import functools

import jax
import jax.numpy as jnp
from jax import lax
from jax.experimental import pallas as pl
from jax.experimental.pallas import tpu as pltpu
from jax.sharding import PartitionSpec as P

MESH = pl.DeviceIdType.MESH
NS_STEPS = 3
COEFF_A, COEFF_B, COEFF_C = (3.4445, -4.775, 2.0315)
UPDATE_SCALE = 0.5
f32, bf16 = jnp.float32, jnp.bfloat16
NN = (((1,), (0,)), ((), ()))
NT = (((1,), (1,)), ((), ()))


def dot(a, b, dims=NN):
    return lax.dot_general(a, b, dims, preferred_element_type=f32)


def split(a):
    high = a.astype(bf16)
    return high, (a - high.astype(f32)).astype(bf16)


def orthogonalize(grads):
    states = [g * lax.rsqrt(jnp.sum(g * g) + 1e-06) for g in grads]
    for _ in range(NS_STEPS):
        parts = [split(x) for x in states]
        grams = [dot(h, h, NT) for h, _ in parts]
        lows = [m.astype(bf16) for m in grams]
        squares = [dot(m, m) for m in lows]
        polys = [split(COEFF_B * m + COEFF_C * s) for m, s in zip(grams, squares)]
        states = [
            COEFF_A * x + (dot(nh, h) + (dot(nh, l) + dot(nl, h)))
            for x, (nh, nl), (h, l) in zip(states, polys, parts)
        ]
    return states


def kernel(
    groups, rows_y, rows_x,
    q_ref, k_ref, v_ref, r_ref, gi_ref, ui_ref, di_ref,
    oq_ref, og_ref, ou_ref, od_ref,
    ke, kbuf, sbuf, rbuf, gbuf, wg, state, wlow, osl, win, oin,
    feed_s, feed_r, rs_s, rs_r, ag_s, ag_r, fw_s, fw_r, in_s, in_r, if_s, if_r, w_s, w_r, o_s, o_r,
):
    chips = rows_y * rows_x
    g = lax.axis_index("group")
    tok = lax.axis_index("tok")
    core = lax.rem(tok, 2)
    chip = tok // 2
    py, px = chip // rows_x, lax.rem(chip, rows_x)
    sib = chip * 2 + (1 - core)
    tokens, width = ke.shape[1], ke.shape[2]
    hid = state.shape[1]
    half = hid // 2
    per = width * half // 128 // chips
    share = wg.shape[2]

    def ring(d, n):
        return min(d, n - d)

    offsets = [(dy, dx) for dy in range(rows_y) for dx in range(rows_x) if (dy, dx) != (0, 0)]
    offsets.sort(key=lambda o: -(ring(o[0], rows_y) + ring(o[1], rows_x)))
    count = len(offsets)

    def ahead(n):
        dy, dx = offsets[n]
        return lax.rem(py + dy, rows_y) * rows_x + lax.rem(px + dx, rows_x)

    def behind(n):
        dy, dx = offsets[n]
        return lax.rem(py + (rows_y - dy), rows_y) * rows_x + lax.rem(px + (rows_x - dx), rows_x)

    def copy(src, dst, send, recv, where):
        return pltpu.make_async_remote_copy(
            src_ref=src, dst_ref=dst, send_sem=send, recv_sem=recv, device_id=where, device_id_type=MESH
        )

    rate = jnp.broadcast_to(r_ref[...].astype(f32), (width, tokens)).T
    ke[0] = k_ref[0]
    ke[1] = (-(rate * v_ref[0].astype(f32))).astype(bf16)

    barrier = pltpu.get_barrier_semaphore()

    def query(weights):
        pre = dot(q_ref[0], weights[0], NT)
        up = dot(q_ref[0], weights[1], NT)
        hidden = (pre * (0.5 + 0.5 * jnp.tanh(0.5 * pre)) * up).astype(bf16)
        oq_ref[0] = dot(hidden, weights[2]).astype(bf16)

    def feed_copy(to):
        return copy(ke, kbuf.at[g, core], feed_s.at[to], feed_r.at[g, core], (0, chip * 2 + to))

    @pl.when(g > 0)
    def _():
        for to in range(2):
            pl.semaphore_signal(barrier, inc=1, device_id=(0, chip * 2 + to), device_id_type=MESH)
        pl.semaphore_wait(barrier, 2)
        feeds = [feed_copy(to) for to in range(2)]
        for f in feeds:
            f.start()
        copy(wlow, win, w_s, w_r, (0, tok)).wait_recv()
        query([win[m] for m in range(3)])
        copy(osl, oin, o_s, o_r, (0, tok)).wait_recv()
        og_ref[0] = oin[0]
        ou_ref[0] = oin[1]
        od_ref[0] = oin[2]
        for f in feeds:
            f.wait_send()

    @pl.when(g == 0)
    def _():
        kbuf[0, core] = ke[...]
        wg[tok, 0] = gi_ref[...]
        wg[tok, 1] = ui_ref[...]
        wg[tok, 2] = di_ref[...]
        for n in range(count):
            pl.semaphore_signal(barrier, inc=1, device_id=(0, ahead(n) * 2 + core), device_id_type=MESH)
        pl.semaphore_signal(barrier, inc=1, device_id=(0, sib), device_id_type=MESH)
        for z in range(1, groups):
            for to in range(2):
                pl.semaphore_signal(barrier, inc=1, device_id=(z, chip * 2 + to), device_id_type=MESH)
        pl.semaphore_wait(barrier, count + 1 + 2 * (groups - 1))

        def first_copy(n):
            return copy(wg.at[tok], wg.at[tok], in_s.at[n], in_r.at[n], (0, ahead(n) * 2 + core))

        def first_pass(n):
            slot = tok if n == count else behind(n) * 2 + core
            return copy(wg.at[slot], wg.at[slot], if_s.at[n], if_r.at[n], (0, sib))

        for n in range(count):
            first_copy(n).start()
        first_pass(count).start()
        feed = copy(ke, kbuf.at[0, core], feed_s.at[0], feed_r.at[0, core], (0, sib))
        feed.start()
        for n in reversed(range(count)):
            first_copy(n).wait_recv()
            first_pass(n).start()
        for n in reversed(range(count + 1)):
            first_pass(n).wait_recv()
        state[0] = wg[:, 0].reshape(width, hid).T
        state[1] = wg[:, 1].reshape(width, hid).T
        state[2] = wg[:, 2].reshape(hid, width)
        wlow[...] = state[...].astype(bf16)
        for n in range(count):
            first_copy(n).wait_send()
        for n in range(count + 1):
            first_pass(n).wait_send()
        feed.wait_send()

        def pick_outgoing():
            rows = lax.broadcasted_iota(jnp.int32, (16, width), 0)
            lanes = lax.broadcasted_iota(jnp.int32, (16, width), 1)
            for part in range(0, share, 16):
                size = min(16, share - part)
                one = jnp.where(lanes == rows + (tok * share + part), 1.0, 0.0).astype(bf16)
                for m in range(2):
                    full = state[m]
                    high, rest = split(full)
                    mid, low = split(full - high.astype(f32))
                    picked = dot(one, high, NT) + (dot(one, mid, NT) + dot(one, low, NT))
                    osl[m, part : part + size, :] = picked[:size]
            osl[2] = state[2, pl.ds(pl.multiple_of(tok * share, share), share), :]

        def slice_copy(n):
            return copy(
                sbuf.at[ahead(n)], rbuf.at[n], rs_s.at[n], rs_r.at[n], (0, ahead(n) * 2 + core)
            )

        def step(i, carry):
            par = lax.rem(i, 2)
            copy(ke, kbuf.at[i, 1 - core], feed_s.at[0], feed_r.at[i, 1 - core], (0, sib)).wait_recv()

            @pl.when(i > 0)
            def _():
                copy(ke, kbuf.at[i, core], feed_s.at[0], feed_r.at[i, core], (0, sib)).wait_recv()

            keys = kbuf[i, :, 0].reshape(2 * tokens, width)
            errs = kbuf[i, :, 1].reshape(2 * tokens, width)
            mine = pl.ds(pl.multiple_of(core * half, half), half)
            pre = dot(wlow[0, mine, :], keys, NT)
            up = dot(wlow[1, mine, :], keys, NT)
            back = dot(wlow[2, mine, :], errs, NT)
            sig = 0.5 + 0.5 * jnp.tanh(0.5 * pre)
            act = pre * sig
            slope = sig + act * (1.0 - sig)
            act_low = (act * up).astype(bf16)
            gate_diff = (back * up * slope).astype(bf16)
            up_diff = (back * act).astype(bf16)
            partial = (dot(gate_diff, keys), dot(up_diff, keys), dot(act_low, errs))
            for m in range(3):
                low = partial[m].astype(bf16)
                for s in range(width // 128):
                    span = chips * 128 // width
                    sbuf[s * span : (s + 1) * span, m] = low[:, s * 128 : (s + 1) * 128].reshape(
                        span, per, 128
                    )
            for n in range(count):
                slice_copy(n).start()

            weights_out = copy(wlow, win, w_s, w_r, (i, tok))
            slices_out = copy(osl, oin, o_s, o_r, (i - 1, tok))

            @pl.when(i == 0)
            def _():
                query([wlow[m] for m in range(3)])

            @pl.when(i > 0)
            def _():
                weights_out.start()
                pick_outgoing()

            @pl.when(i == 1)
            def _():
                og_ref[0] = osl[0]
                ou_ref[0] = osl[1]
                od_ref[0] = osl[2]

            @pl.when(i > 1)
            def _():
                slices_out.start()

            for n in reversed(range(count)):
                slice_copy(n).wait_recv()
            total = sbuf[chip].astype(f32)
            for n in range(count):
                total = total + rbuf[n].astype(f32)
            gbuf[par, core, chip] = total.astype(bf16)

            def sum_copy(n):
                slot = gbuf.at[par, core, chip]
                return copy(slot, slot, ag_s.at[n], ag_r.at[n], (0, ahead(n) * 2 + core))

            def pass_copy(n):
                slot = gbuf.at[par, core, chip if n == count else behind(n)]
                return copy(slot, slot, fw_s.at[n], fw_r.at[par, n], (0, sib))

            for n in range(count):
                sum_copy(n).start()
            pass_copy(count).start()
            for n in reversed(range(count)):
                sum_copy(n).wait_recv()
                pass_copy(n).start()
            for n in reversed(range(count + 1)):
                pass_copy(n).wait_recv()

            grads = []
            for m in range(3):
                sides = []
                for c in range(2):
                    span = chips * 128 // width
                    sides.append(
                        jnp.concatenate(
                            [
                                gbuf[par, c, s * span : (s + 1) * span, m].reshape(half, 128)
                                for s in range(width // 128)
                            ],
                            axis=1,
                        )
                    )
                grads.append(jnp.concatenate(sides, axis=0).astype(f32))
            ortho = orthogonalize(grads)

            for n in range(count):
                slice_copy(n).wait_send()
                sum_copy(n).wait_send()
            for n in range(count + 1):
                pass_copy(n).wait_send()

            @pl.when(i > 0)
            def _():
                weights_out.wait_send()

            @pl.when(i > 1)
            def _():
                slices_out.wait_send()

            for m in range(3):
                before = state[m]
                stepped = before - UPDATE_SCALE * ortho[m]
                axis = 0 if m == 2 else 1
                target = jnp.sum(before * before, axis=axis, keepdims=True)
                present = jnp.sum(stepped * stepped, axis=axis, keepdims=True)
                after = stepped * (jnp.sqrt(target) * lax.rsqrt(present + 1e-06))
                state[m] = after
                wlow[m] = after.astype(bf16)
            return carry

        lax.fori_loop(0, groups, step, 0)
        pick_outgoing()
        last = copy(osl, oin, o_s, o_r, (groups - 1, tok))
        last.start()
        last.wait_send()


def solution(mesh):
    groups, devices = mesh.shape["group"], mesh.shape["tok"]
    chips = devices // 2
    rows_y = 4 if chips == 16 else 2
    rows_x = chips // rows_y

    def body(query_rows, key_rows, value_rows, token_rates, gate_init, up_init, down_init):
        tokens, width = key_rows.shape[1:]
        share, hid = gate_init.shape
        share_w = down_init.shape[0]
        per = width * (hid // 2) // 128 // chips
        count = chips - 1
        vmem = pl.BlockSpec(memory_space=pltpu.VMEM)
        dma = pltpu.SemaphoreType.DMA
        return pl.pallas_call(
            functools.partial(kernel, groups, rows_y, rows_x),
            out_shape=(
                jax.ShapeDtypeStruct((1, tokens, width), bf16),
                jax.ShapeDtypeStruct((1, share, hid), f32),
                jax.ShapeDtypeStruct((1, share, hid), f32),
                jax.ShapeDtypeStruct((1, share_w, width), f32),
            ),
            in_specs=[vmem] * 7,
            out_specs=(vmem,) * 4,
            scratch_shapes=[
                pltpu.VMEM((2, tokens, width), bf16),
                pltpu.VMEM((groups, 2, 2, tokens, width), bf16),
                pltpu.VMEM((chips, 3, per, 128), bf16),
                pltpu.VMEM((count, 3, per, 128), bf16),
                pltpu.VMEM((2, 2, chips, 3, per, 128), bf16),
                pltpu.VMEM((devices, 3, share, hid), f32),
                pltpu.VMEM((3, hid, width), f32),
                pltpu.VMEM((3, hid, width), bf16),
                pltpu.VMEM((3, share, hid), f32),
                pltpu.VMEM((3, hid, width), bf16),
                pltpu.VMEM((3, share, hid), f32),
                dma((2,)),
                dma((groups, 2)),
                dma((count,)),
                dma((count,)),
                dma((count,)),
                dma((count,)),
                dma((chips,)),
                dma((2, chips)),
                dma((count,)),
                dma((count,)),
                dma((chips,)),
                dma((chips,)),
                dma,
                dma,
                dma,
                dma,
            ],
            compiler_params=pltpu.CompilerParams(
                collective_id=0, has_side_effects=True, vmem_limit_bytes=48 * 1024 * 1024
            ),
            cost_estimate=pl.CostEstimate(flops=10**10, bytes_accessed=10**7, transcendentals=10**6),
        )(query_rows, key_rows, value_rows, token_rates, gate_init, up_init, down_init)

    rows = P("group", "tok", None)
    return jax.shard_map(
        body,
        mesh=mesh,
        in_specs=(rows, rows, rows, P("group", "tok"), P("tok", None), P("tok", None), P("tok", None)),
        out_specs=(rows, rows, rows, rows),
        check_vma=False,
    )
```

```python
import functools

import jax
import jax.numpy as jnp
from jax import lax
from jax.experimental import pallas as pl
from jax.experimental.pallas import tpu as pltpu
from jax.sharding import PartitionSpec as P

MESH = pl.DeviceIdType.MESH
NS_STEPS = 3
COEFF_A, COEFF_B, COEFF_C = (3.4445, -4.775, 2.0315)
UPDATE_SCALE = 0.5
f32, bf16 = jnp.float32, jnp.bfloat16
NN = (((1,), (0,)), ((), ()))
NT = (((1,), (1,)), ((), ()))


def dot(a, b, dims=NN):
    return lax.dot_general(a, b, dims, preferred_element_type=f32)


def split(a):
    high = a.astype(bf16)
    return high, (a - high.astype(f32)).astype(bf16)


def orthogonalize(grads):
    states = [g * lax.rsqrt(jnp.sum(g * g) + 1e-06) for g in grads]
    for _ in range(NS_STEPS):
        parts = [split(x) for x in states]
        grams = [dot(h, h, NT) for h, _ in parts]
        lows = [m.astype(bf16) for m in grams]
        squares = [dot(m, m) for m in lows]
        polys = [split(COEFF_B * m + COEFF_C * s) for m, s in zip(grams, squares)]
        states = [
            COEFF_A * x + (dot(nh, h) + (dot(nh, l) + dot(nl, h)))
            for x, (nh, nl), (h, l) in zip(states, polys, parts)
        ]
    return states


def kernel(
    groups, rows_y, rows_x,
    q_ref, k_ref, v_ref, r_ref, gi_ref, ui_ref, di_ref,
    oq_ref, og_ref, ou_ref, od_ref,
    qbuf, vbuf, rates, ke, kbuf, sbuf, rbuf, gbuf, wg, state, wlow, osl, win, oin,
    load, feed_s, feed_r, rs_s, rs_r, ag_s, ag_r, fw_s, fw_r, in_s, in_r, if_s, if_r, w_s, w_r, o_s, o_r,
):
    chips = rows_y * rows_x
    g = lax.axis_index("group")
    tok = lax.axis_index("tok")
    core = lax.rem(tok, 2)
    chip = tok // 2
    py, px = chip // rows_x, lax.rem(chip, rows_x)
    sib = chip * 2 + (1 - core)
    tokens, width = ke.shape[1], ke.shape[2]
    hid = state.shape[1]
    half = hid // 2
    per = width * half // 128 // chips
    share = wg.shape[2]

    def ring(d, n):
        return min(d, n - d)

    offsets = [(dy, dx) for dy in range(rows_y) for dx in range(rows_x) if (dy, dx) != (0, 0)]
    offsets.sort(key=lambda o: -(ring(o[0], rows_y) + ring(o[1], rows_x)))
    count = len(offsets)

    def ahead(n):
        dy, dx = offsets[n]
        return lax.rem(py + dy, rows_y) * rows_x + lax.rem(px + dx, rows_x)

    def behind(n):
        dy, dx = offsets[n]
        return lax.rem(py + (rows_y - dy), rows_y) * rows_x + lax.rem(px + (rows_x - dx), rows_x)

    def copy(src, dst, send, recv, where):
        return pltpu.make_async_remote_copy(
            src_ref=src, dst_ref=dst, send_sem=send, recv_sem=recv, device_id=where, device_id_type=MESH
        )

    loads = [
        pltpu.make_async_copy(v_ref.at[0], vbuf, load.at[0]),
        pltpu.make_async_copy(r_ref, rates, load.at[1]),
        pltpu.make_async_copy(k_ref.at[0], ke.at[0], load.at[2]),
        pltpu.make_async_copy(q_ref.at[0], qbuf, load.at[3]),
    ]
    barrier = pltpu.get_barrier_semaphore()

    def scale_values():
        for n in range(3):
            loads[n].wait()
        rate = jnp.broadcast_to(rates[...].astype(f32), (width, tokens)).T
        ke[1] = (-(rate * vbuf[...].astype(f32))).astype(bf16)

    def query(weights):
        pre = dot(qbuf[...], weights[0], NT)
        up = dot(qbuf[...], weights[1], NT)
        hidden = (pre * (0.5 + 0.5 * jnp.tanh(0.5 * pre)) * up).astype(bf16)
        oq_ref[0] = dot(hidden, weights[2]).astype(bf16)

    @pl.when(g > 0)
    def _():
        pl.semaphore_signal(barrier, inc=1, device_id=(0, tok), device_id_type=MESH)
        for n in range(4):
            loads[n].start()
        scale_values()
        pl.semaphore_wait(barrier, 1)
        feed = copy(ke, kbuf.at[g, core], feed_s, feed_r.at[g, core], (0, tok))
        feed.start()
        loads[3].wait()
        copy(wlow, win, w_s, w_r, (0, tok)).wait_recv()
        query([win[m] for m in range(3)])
        copy(osl, oin, o_s, o_r, (0, tok)).wait_recv()
        og_ref[0] = oin[0]
        ou_ref[0] = oin[1]
        od_ref[0] = oin[2]
        feed.wait_send()

    @pl.when(g == 0)
    def _():
        firsts = [
            pltpu.make_async_copy(ref, wg.at[tok, m], load.at[4 + m])
            for m, ref in enumerate((gi_ref, ui_ref, di_ref))
        ]
        for c in firsts:
            c.start()
        for n in range(4):
            loads[n].start()
        for n in range(count):
            pl.semaphore_signal(barrier, inc=1, device_id=(0, ahead(n) * 2 + core), device_id_type=MESH)
        pl.semaphore_signal(barrier, inc=1, device_id=(0, sib), device_id_type=MESH)
        for z in range(1, groups):
            pl.semaphore_signal(barrier, inc=1, device_id=(z, tok), device_id_type=MESH)
        for c in firsts:
            c.wait()
        pl.semaphore_wait(barrier, count + groups)

        def first_copy(n):
            return copy(wg.at[tok], wg.at[tok], in_s.at[n], in_r.at[n], (0, ahead(n) * 2 + core))

        def first_pass(n):
            slot = tok if n == count else behind(n) * 2 + core
            return copy(wg.at[slot], wg.at[slot], if_s.at[n], if_r.at[n], (0, sib))

        for n in range(count):
            first_copy(n).start()
        first_pass(count).start()
        scale_values()
        kbuf[0, core] = ke[...]
        feed = copy(ke, kbuf.at[0, core], feed_s, feed_r.at[0, core], (0, sib))
        feed.start()
        loads[3].wait()
        for n in reversed(range(count)):
            first_copy(n).wait_recv()
            first_pass(n).start()
        for n in reversed(range(count + 1)):
            first_pass(n).wait_recv()
        state[0] = wg[:, 0].reshape(width, hid).T
        state[1] = wg[:, 1].reshape(width, hid).T
        state[2] = wg[:, 2].reshape(hid, width)
        wlow[...] = state[...].astype(bf16)
        for n in range(count):
            first_copy(n).wait_send()
        for n in range(count + 1):
            first_pass(n).wait_send()
        feed.wait_send()

        def pick_outgoing():
            rows = lax.broadcasted_iota(jnp.int32, (16, width), 0)
            lanes = lax.broadcasted_iota(jnp.int32, (16, width), 1)
            for part in range(0, share, 16):
                size = min(16, share - part)
                one = jnp.where(lanes == rows + (tok * share + part), 1.0, 0.0).astype(bf16)
                for m in range(2):
                    full = state[m]
                    high, rest = split(full)
                    mid, low = split(full - high.astype(f32))
                    picked = dot(one, high, NT) + (dot(one, mid, NT) + dot(one, low, NT))
                    osl[m, part : part + size, :] = picked[:size]
            osl[2] = state[2, pl.ds(pl.multiple_of(tok * share, share), share), :]

        def slice_copy(n):
            return copy(
                sbuf.at[ahead(n)], rbuf.at[n], rs_s.at[n], rs_r.at[n], (0, ahead(n) * 2 + core)
            )

        def step(i, carry):
            par = lax.rem(i, 2)
            copy(ke, kbuf.at[i, 1 - core], feed_s, feed_r.at[i, 1 - core], (0, sib)).wait_recv()
            keys = kbuf[i, :, 0].reshape(2 * tokens, width)
            errs = kbuf[i, :, 1].reshape(2 * tokens, width)
            mine = pl.ds(pl.multiple_of(core * half, half), half)
            pre = dot(wlow[0, mine, :], keys, NT)
            up = dot(wlow[1, mine, :], keys, NT)
            back = dot(wlow[2, mine, :], errs, NT)
            sig = 0.5 + 0.5 * jnp.tanh(0.5 * pre)
            act = pre * sig
            slope = sig + act * (1.0 - sig)
            act_low = (act * up).astype(bf16)
            gate_diff = (back * up * slope).astype(bf16)
            up_diff = (back * act).astype(bf16)
            partial = (dot(gate_diff, keys), dot(up_diff, keys), dot(act_low, errs))
            for m in range(3):
                low = partial[m].astype(bf16)
                for s in range(width // 128):
                    span = chips * 128 // width
                    sbuf[s * span : (s + 1) * span, m] = low[:, s * 128 : (s + 1) * 128].reshape(
                        span, per, 128
                    )
            for n in range(count):
                slice_copy(n).start()

            weights_out = copy(wlow, win, w_s, w_r, (i, tok))
            slices_out = copy(osl, oin, o_s, o_r, (i - 1, tok))

            @pl.when(i == 0)
            def _():
                query([wlow[m] for m in range(3)])

            @pl.when(i > 0)
            def _():
                weights_out.start()
                pick_outgoing()

            @pl.when(i == 1)
            def _():
                og_ref[0] = osl[0]
                ou_ref[0] = osl[1]
                od_ref[0] = osl[2]

            @pl.when(i > 1)
            def _():
                slices_out.start()

            for n in reversed(range(count)):
                slice_copy(n).wait_recv()
            total = sbuf[chip].astype(f32)
            for n in range(count):
                total = total + rbuf[n].astype(f32)
            gbuf[par, core, chip] = total.astype(bf16)

            def sum_copy(n):
                slot = gbuf.at[par, core, chip]
                return copy(slot, slot, ag_s.at[n], ag_r.at[n], (0, ahead(n) * 2 + core))

            def pass_copy(n):
                slot = gbuf.at[par, core, chip if n == count else behind(n)]
                return copy(slot, slot, fw_s.at[n], fw_r.at[par, n], (0, sib))

            for n in range(count):
                sum_copy(n).start()
            pass_copy(count).start()
            for n in reversed(range(count)):
                sum_copy(n).wait_recv()
                pass_copy(n).start()
            for n in reversed(range(count + 1)):
                pass_copy(n).wait_recv()

            coming = jnp.minimum(i + 1, groups - 1)
            pass_feed = copy(
                kbuf.at[coming, core], kbuf.at[coming, core], feed_s, feed_r.at[coming, core], (0, sib)
            )

            @pl.when(i < groups - 1)
            def _():
                pass_feed.wait_recv()
                pass_feed.start()

            grads = []
            for m in range(3):
                sides = []
                for c in range(2):
                    span = chips * 128 // width
                    sides.append(
                        jnp.concatenate(
                            [
                                gbuf[par, c, s * span : (s + 1) * span, m].reshape(half, 128)
                                for s in range(width // 128)
                            ],
                            axis=1,
                        )
                    )
                grads.append(jnp.concatenate(sides, axis=0).astype(f32))
            ortho = orthogonalize(grads)

            @pl.when(i < groups - 1)
            def _():
                pass_feed.wait_send()

            for n in range(count):
                slice_copy(n).wait_send()
                sum_copy(n).wait_send()
            for n in range(count + 1):
                pass_copy(n).wait_send()

            @pl.when(i > 0)
            def _():
                weights_out.wait_send()

            @pl.when(i > 1)
            def _():
                slices_out.wait_send()

            for m in range(3):
                before = state[m]
                stepped = before - UPDATE_SCALE * ortho[m]
                axis = 0 if m == 2 else 1
                target = jnp.sum(before * before, axis=axis, keepdims=True)
                present = jnp.sum(stepped * stepped, axis=axis, keepdims=True)
                after = stepped * (jnp.sqrt(target) * lax.rsqrt(present + 1e-06))
                state[m] = after
                wlow[m] = after.astype(bf16)
            return carry

        lax.fori_loop(0, groups, step, 0)
        pick_outgoing()
        last = copy(osl, oin, o_s, o_r, (groups - 1, tok))
        last.start()
        last.wait_send()


def solution(mesh):
    groups, devices = mesh.shape["group"], mesh.shape["tok"]
    chips = devices // 2
    rows_y = 4 if chips == 16 else 2
    rows_x = chips // rows_y

    def body(query_rows, key_rows, value_rows, token_rates, gate_init, up_init, down_init):
        tokens, width = key_rows.shape[1:]
        share, hid = gate_init.shape
        share_w = down_init.shape[0]
        per = width * (hid // 2) // 128 // chips
        count = chips - 1
        vmem = pl.BlockSpec(memory_space=pltpu.VMEM)
        dma = pltpu.SemaphoreType.DMA
        return pl.pallas_call(
            functools.partial(kernel, groups, rows_y, rows_x),
            out_shape=(
                jax.ShapeDtypeStruct((1, tokens, width), bf16),
                jax.ShapeDtypeStruct((1, share, hid), f32),
                jax.ShapeDtypeStruct((1, share, hid), f32),
                jax.ShapeDtypeStruct((1, share_w, width), f32),
            ),
            in_specs=[pl.BlockSpec(memory_space=pltpu.MemorySpace.HBM)] * 7,
            out_specs=(vmem,) * 4,
            scratch_shapes=[
                pltpu.VMEM((tokens, width), bf16),
                pltpu.VMEM((tokens, width), bf16),
                pltpu.VMEM((1, tokens), bf16),
                pltpu.VMEM((2, tokens, width), bf16),
                pltpu.VMEM((groups, 2, 2, tokens, width), bf16),
                pltpu.VMEM((chips, 3, per, 128), bf16),
                pltpu.VMEM((count, 3, per, 128), bf16),
                pltpu.VMEM((2, 2, chips, 3, per, 128), bf16),
                pltpu.VMEM((devices, 3, share, hid), f32),
                pltpu.VMEM((3, hid, width), f32),
                pltpu.VMEM((3, hid, width), bf16),
                pltpu.VMEM((3, share, hid), f32),
                pltpu.VMEM((3, hid, width), bf16),
                pltpu.VMEM((3, share, hid), f32),
                dma((7,)),
                dma,
                dma((groups, 2)),
                dma((count,)),
                dma((count,)),
                dma((count,)),
                dma((count,)),
                dma((chips,)),
                dma((2, chips)),
                dma((count,)),
                dma((count,)),
                dma((chips,)),
                dma((chips,)),
                dma,
                dma,
                dma,
                dma,
            ],
            compiler_params=pltpu.CompilerParams(
                collective_id=0, has_side_effects=True, vmem_limit_bytes=63 * 1024 * 1024
            ),
            cost_estimate=pl.CostEstimate(flops=10**10, bytes_accessed=10**7, transcendentals=10**6),
        )(query_rows, key_rows, value_rows, token_rates, gate_init, up_init, down_init)

    rows = P("group", "tok", None)
    return jax.shard_map(
        body,
        mesh=mesh,
        in_specs=(rows, rows, rows, P("group", "tok"), P("tok", None), P("tok", None), P("tok", None)),
        out_specs=(rows, rows, rows, rows),
        check_vma=False,
    )
```

```python
import functools

import jax
import jax.numpy as jnp
from jax import lax
from jax.experimental import pallas as pl
from jax.experimental.pallas import tpu as pltpu
from jax.sharding import PartitionSpec as P

MESH = pl.DeviceIdType.MESH
NS_STEPS = 3
COEFF_A, COEFF_B, COEFF_C = (3.4445, -4.775, 2.0315)
UPDATE_SCALE = 0.5
f32, bf16 = jnp.float32, jnp.bfloat16
NN = (((1,), (0,)), ((), ()))
NT = (((1,), (1,)), ((), ()))


def dot(a, b, dims=NN):
    return lax.dot_general(a, b, dims, preferred_element_type=f32)


def split(a):
    high = a.astype(bf16)
    return high, (a - high.astype(f32)).astype(bf16)


def orthogonalize(grads):
    states = [g * lax.rsqrt(jnp.sum(g * g) + 1e-06) for g in grads]
    for repeat in range(NS_STEPS):
        highs = [x.astype(bf16) for x in states]
        grams = [dot(h, h, NT) for h in highs]
        lows = [m.astype(bf16) for m in grams]
        squares = [dot(m, m) for m in lows]
        polys = [COEFF_B * m + COEFF_C * s for m, s in zip(grams, squares)]
        if repeat + 1 < NS_STEPS:
            moves = [dot(p.astype(bf16), h) for p, h in zip(polys, highs)]
        else:
            moves = []
            for p, x in zip(polys, states):
                (ph, pl_), (xh, xl) = split(p), split(x)
                moves.append(dot(ph, xh) + (dot(ph, xl) + dot(pl_, xh)))
        states = [COEFF_A * x + m for x, m in zip(states, moves)]
    return states


def kernel(
    groups, rows_y, rows_x,
    q_ref, k_ref, v_ref, r_ref, gi_ref, ui_ref, di_ref,
    oq_ref, og_ref, ou_ref, od_ref,
    qbuf, vbuf, rates, ke, kbuf, sbuf, rbuf, gbuf, wg, state, wlow, osl, win, oin,
    load, feed_s, feed_r, rs_s, rs_r, ag_s, ag_r, fw_s, fw_r, in_s, in_r, if_s, if_r, w_s, w_r, o_s, o_r,
):
    chips = rows_y * rows_x
    g = lax.axis_index("group")
    tok = lax.axis_index("tok")
    core = lax.rem(tok, 2)
    chip = tok // 2
    py, px = chip // rows_x, lax.rem(chip, rows_x)
    sib = chip * 2 + (1 - core)
    tokens, width = ke.shape[1], ke.shape[2]
    hid = state.shape[1]
    half = hid // 2
    per = width * half // 128 // chips
    share = wg.shape[2]

    def ring(d, n):
        return min(d, n - d)

    offsets = [(dy, dx) for dy in range(rows_y) for dx in range(rows_x) if (dy, dx) != (0, 0)]
    offsets.sort(key=lambda o: -(ring(o[0], rows_y) + ring(o[1], rows_x)))
    count = len(offsets)

    def ahead(n):
        dy, dx = offsets[n]
        return lax.rem(py + dy, rows_y) * rows_x + lax.rem(px + dx, rows_x)

    def behind(n):
        dy, dx = offsets[n]
        return lax.rem(py + (rows_y - dy), rows_y) * rows_x + lax.rem(px + (rows_x - dx), rows_x)

    def copy(src, dst, send, recv, where):
        return pltpu.make_async_remote_copy(
            src_ref=src, dst_ref=dst, send_sem=send, recv_sem=recv, device_id=where, device_id_type=MESH
        )

    loads = [
        pltpu.make_async_copy(v_ref.at[0], vbuf, load.at[0]),
        pltpu.make_async_copy(r_ref, rates, load.at[1]),
        pltpu.make_async_copy(k_ref.at[0], ke.at[0], load.at[2]),
        pltpu.make_async_copy(q_ref.at[0], qbuf, load.at[3]),
    ]
    barrier = pltpu.get_barrier_semaphore()

    def scale_values():
        for n in range(3):
            loads[n].wait()
        rate = jnp.broadcast_to(rates[...].astype(f32), (width, tokens)).T
        ke[1] = (-(rate * vbuf[...].astype(f32))).astype(bf16)

    def query(weights):
        pre = dot(qbuf[...], weights[0], NT)
        up = dot(qbuf[...], weights[1], NT)
        hidden = (pre * (0.5 + 0.5 * jnp.tanh(0.5 * pre)) * up).astype(bf16)
        oq_ref[0] = dot(hidden, weights[2]).astype(bf16)

    @pl.when(g > 0)
    def _():
        pl.semaphore_signal(barrier, inc=1, device_id=(0, tok), device_id_type=MESH)
        for n in range(4):
            loads[n].start()
        scale_values()
        pl.semaphore_wait(barrier, 1)
        feed = copy(ke, kbuf.at[g, core], feed_s, feed_r.at[g, core], (0, tok))
        feed.start()
        loads[3].wait()
        copy(wlow, win, w_s, w_r, (0, tok)).wait_recv()
        query([win[m] for m in range(3)])
        copy(osl, oin, o_s, o_r, (0, tok)).wait_recv()
        og_ref[0] = oin[0]
        ou_ref[0] = oin[1]
        od_ref[0] = oin[2]
        feed.wait_send()

    @pl.when(g == 0)
    def _():
        firsts = [
            pltpu.make_async_copy(ref, wg.at[tok, m], load.at[4 + m])
            for m, ref in enumerate((gi_ref, ui_ref, di_ref))
        ]
        for c in firsts:
            c.start()
        for n in range(4):
            loads[n].start()
        for n in range(count):
            pl.semaphore_signal(barrier, inc=1, device_id=(0, ahead(n) * 2 + core), device_id_type=MESH)
        pl.semaphore_signal(barrier, inc=1, device_id=(0, sib), device_id_type=MESH)
        for z in range(1, groups):
            pl.semaphore_signal(barrier, inc=1, device_id=(z, tok), device_id_type=MESH)
        for c in firsts:
            c.wait()
        pl.semaphore_wait(barrier, count + groups)

        def first_copy(n):
            return copy(wg.at[tok], wg.at[tok], in_s.at[n], in_r.at[n], (0, ahead(n) * 2 + core))

        def first_pass(n):
            slot = tok if n == count else behind(n) * 2 + core
            return copy(wg.at[slot], wg.at[slot], if_s.at[n], if_r.at[n], (0, sib))

        for n in range(count):
            first_copy(n).start()
        first_pass(count).start()
        scale_values()
        kbuf[0, core] = ke[...]
        feed = copy(ke, kbuf.at[0, core], feed_s, feed_r.at[0, core], (0, sib))
        feed.start()
        loads[3].wait()
        for n in reversed(range(count)):
            first_copy(n).wait_recv()
            first_pass(n).start()
        for n in reversed(range(count + 1)):
            first_pass(n).wait_recv()
        state[0] = wg[:, 0].reshape(width, hid).T
        state[1] = wg[:, 1].reshape(width, hid).T
        state[2] = wg[:, 2].reshape(hid, width)
        wlow[...] = state[...].astype(bf16)
        for n in range(count):
            first_copy(n).wait_send()
        for n in range(count + 1):
            first_pass(n).wait_send()
        feed.wait_send()

        def pick_outgoing():
            rows = lax.broadcasted_iota(jnp.int32, (16, width), 0)
            lanes = lax.broadcasted_iota(jnp.int32, (16, width), 1)
            for part in range(0, share, 16):
                size = min(16, share - part)
                one = jnp.where(lanes == rows + (tok * share + part), 1.0, 0.0).astype(bf16)
                for m in range(2):
                    full = state[m]
                    high, rest = split(full)
                    mid, low = split(full - high.astype(f32))
                    picked = dot(one, high, NT) + (dot(one, mid, NT) + dot(one, low, NT))
                    osl[m, part : part + size, :] = picked[:size]
            osl[2] = state[2, pl.ds(pl.multiple_of(tok * share, share), share), :]

        def slice_copy(n):
            return copy(
                sbuf.at[ahead(n)], rbuf.at[n], rs_s.at[n], rs_r.at[n], (0, ahead(n) * 2 + core)
            )

        def sum_copy(par, n):
            slot = gbuf.at[par, core, chip]
            return copy(slot, slot, ag_s.at[n], ag_r.at[n], (0, ahead(n) * 2 + core))

        def pass_copy(par, n):
            slot = gbuf.at[par, core, chip if n == count else behind(n)]
            return copy(slot, slot, fw_s.at[n], fw_r.at[par, n], (0, sib))

        def sums_sent(par):
            for n in range(count):
                sum_copy(par, n).wait_send()
            for n in range(count + 1):
                pass_copy(par, n).wait_send()

        def step(i, carry):
            par = lax.rem(i, 2)
            copy(ke, kbuf.at[i, 1 - core], feed_s, feed_r.at[i, 1 - core], (0, sib)).wait_recv()
            keys = kbuf[i, :, 0].reshape(2 * tokens, width)
            errs = kbuf[i, :, 1].reshape(2 * tokens, width)
            mine = pl.ds(pl.multiple_of(core * half, half), half)
            pre = dot(wlow[0, mine, :], keys, NT)
            up = dot(wlow[1, mine, :], keys, NT)
            back = dot(wlow[2, mine, :], errs, NT)
            sig = 0.5 + 0.5 * jnp.tanh(0.5 * pre)
            act = pre * sig
            slope = sig + act * (1.0 - sig)
            act_low = (act * up).astype(bf16)
            gate_diff = (back * up * slope).astype(bf16)
            up_diff = (back * act).astype(bf16)
            partial = (dot(gate_diff, keys), dot(up_diff, keys), dot(act_low, errs))
            for m in range(3):
                low = partial[m].astype(bf16)
                for s in range(width // 128):
                    span = chips * 128 // width
                    sbuf[s * span : (s + 1) * span, m] = low[:, s * 128 : (s + 1) * 128].reshape(
                        span, per, 128
                    )
            for n in range(count):
                slice_copy(n).start()

            weights_out = copy(wlow, win, w_s, w_r, (i, tok))
            slices_out = copy(osl, oin, o_s, o_r, (i - 1, tok))

            @pl.when(i == 0)
            def _():
                query([wlow[m] for m in range(3)])

            @pl.when(i > 0)
            def _():
                weights_out.start()
                pick_outgoing()
                sums_sent(1 - par)

            @pl.when(i == 1)
            def _():
                og_ref[0] = osl[0]
                ou_ref[0] = osl[1]
                od_ref[0] = osl[2]

            @pl.when(i > 1)
            def _():
                slices_out.start()

            for n in reversed(range(count)):
                slice_copy(n).wait_recv()
            total = sbuf[chip].astype(f32)
            for n in range(count):
                total = total + rbuf[n].astype(f32)
            gbuf[par, core, chip] = total.astype(bf16)

            for n in range(count):
                sum_copy(par, n).start()
            pass_copy(par, count).start()
            for n in range(count):
                slice_copy(n).wait_send()
            for n in reversed(range(count)):
                sum_copy(par, n).wait_recv()
                pass_copy(par, n).start()
            for n in reversed(range(count + 1)):
                pass_copy(par, n).wait_recv()

            coming = jnp.minimum(i + 1, groups - 1)
            pass_feed = copy(
                kbuf.at[coming, core], kbuf.at[coming, core], feed_s, feed_r.at[coming, core], (0, sib)
            )

            @pl.when(i < groups - 1)
            def _():
                pass_feed.wait_recv()
                pass_feed.start()

            grads = []
            for m in range(3):
                sides = []
                for c in range(2):
                    span = chips * 128 // width
                    sides.append(
                        jnp.concatenate(
                            [
                                gbuf[par, c, s * span : (s + 1) * span, m].reshape(half, 128)
                                for s in range(width // 128)
                            ],
                            axis=1,
                        )
                    )
                grads.append(jnp.concatenate(sides, axis=0).astype(f32))
            ortho = orthogonalize(grads)

            @pl.when(i < groups - 1)
            def _():
                pass_feed.wait_send()

            @pl.when(i > 0)
            def _():
                weights_out.wait_send()

            @pl.when(i > 1)
            def _():
                slices_out.wait_send()

            for m in range(3):
                before = state[m]
                stepped = before - UPDATE_SCALE * ortho[m]
                axis = 0 if m == 2 else 1
                target = jnp.sum(before * before, axis=axis, keepdims=True)
                present = jnp.sum(stepped * stepped, axis=axis, keepdims=True)
                after = stepped * (jnp.sqrt(target) * lax.rsqrt(present + 1e-06))
                state[m] = after
                wlow[m] = after.astype(bf16)
            return carry

        lax.fori_loop(0, groups, step, 0)
        pick_outgoing()
        last = copy(osl, oin, o_s, o_r, (groups - 1, tok))
        last.start()
        sums_sent((groups - 1) % 2)
        last.wait_send()


def solution(mesh):
    groups, devices = mesh.shape["group"], mesh.shape["tok"]
    chips = devices // 2
    rows_y = 4 if chips == 16 else 2
    rows_x = chips // rows_y

    def body(query_rows, key_rows, value_rows, token_rates, gate_init, up_init, down_init):
        tokens, width = key_rows.shape[1:]
        share, hid = gate_init.shape
        share_w = down_init.shape[0]
        per = width * (hid // 2) // 128 // chips
        count = chips - 1
        vmem = pl.BlockSpec(memory_space=pltpu.VMEM)
        dma = pltpu.SemaphoreType.DMA
        return pl.pallas_call(
            functools.partial(kernel, groups, rows_y, rows_x),
            out_shape=(
                jax.ShapeDtypeStruct((1, tokens, width), bf16),
                jax.ShapeDtypeStruct((1, share, hid), f32),
                jax.ShapeDtypeStruct((1, share, hid), f32),
                jax.ShapeDtypeStruct((1, share_w, width), f32),
            ),
            in_specs=[pl.BlockSpec(memory_space=pltpu.MemorySpace.HBM)] * 7,
            out_specs=(vmem,) * 4,
            scratch_shapes=[
                pltpu.VMEM((tokens, width), bf16),
                pltpu.VMEM((tokens, width), bf16),
                pltpu.VMEM((1, tokens), bf16),
                pltpu.VMEM((2, tokens, width), bf16),
                pltpu.VMEM((groups, 2, 2, tokens, width), bf16),
                pltpu.VMEM((chips, 3, per, 128), bf16),
                pltpu.VMEM((count, 3, per, 128), bf16),
                pltpu.VMEM((2, 2, chips, 3, per, 128), bf16),
                pltpu.VMEM((devices, 3, share, hid), f32),
                pltpu.VMEM((3, hid, width), f32),
                pltpu.VMEM((3, hid, width), bf16),
                pltpu.VMEM((3, share, hid), f32),
                pltpu.VMEM((3, hid, width), bf16),
                pltpu.VMEM((3, share, hid), f32),
                dma((7,)),
                dma,
                dma((groups, 2)),
                dma((count,)),
                dma((count,)),
                dma((count,)),
                dma((count,)),
                dma((chips,)),
                dma((2, chips)),
                dma((count,)),
                dma((count,)),
                dma((chips,)),
                dma((chips,)),
                dma,
                dma,
                dma,
                dma,
            ],
            compiler_params=pltpu.CompilerParams(
                collective_id=0, has_side_effects=True, vmem_limit_bytes=63 * 1024 * 1024
            ),
            cost_estimate=pl.CostEstimate(flops=10**10, bytes_accessed=10**7, transcendentals=10**6),
        )(query_rows, key_rows, value_rows, token_rates, gate_init, up_init, down_init)

    rows = P("group", "tok", None)
    return jax.shard_map(
        body,
        mesh=mesh,
        in_specs=(rows, rows, rows, P("group", "tok"), P("tok", None), P("tok", None), P("tok", None)),
        out_specs=(rows, rows, rows, rows),
        check_vma=False,
    )
```

```python
import functools

import jax
import jax.numpy as jnp
from jax import lax
from jax.experimental import pallas as pl
from jax.experimental.pallas import tpu as pltpu
from jax.sharding import PartitionSpec as P

MESH = pl.DeviceIdType.MESH
NS_STEPS = 3
COEFF_A, COEFF_B, COEFF_C = (3.4445, -4.775, 2.0315)
UPDATE_SCALE = 0.5
f32, bf16 = jnp.float32, jnp.bfloat16
NN = (((1,), (0,)), ((), ()))
NT = (((1,), (1,)), ((), ()))


def dot(a, b, dims=NN):
    return lax.dot_general(a, b, dims, preferred_element_type=f32)


def split(a):
    high = a.astype(bf16)
    return high, (a - high.astype(f32)).astype(bf16)


def orthogonalize(grads):
    states = [g * lax.rsqrt(jnp.sum(g * g) + 1e-06) for g in grads]
    for repeat in range(NS_STEPS):
        highs = [x.astype(bf16) for x in states]
        grams = [dot(h, h, NT) for h in highs]
        lows = [m.astype(bf16) for m in grams]
        squares = [dot(m, m) for m in lows]
        polys = [COEFF_B * m + COEFF_C * s for m, s in zip(grams, squares)]
        if repeat + 1 < NS_STEPS:
            moves = [dot(p.astype(bf16), h) for p, h in zip(polys, highs)]
        else:
            moves = []
            for p, x in zip(polys, states):
                (ph, pl_), (xh, xl) = split(p), split(x)
                moves.append(dot(ph, xh) + (dot(ph, xl) + dot(pl_, xh)))
        states = [COEFF_A * x + m for x, m in zip(states, moves)]
    return states


def kernel(
    groups, rows_y, rows_x,
    q_ref, k_ref, v_ref, r_ref, gi_ref, ui_ref, di_ref,
    oq_ref, og_ref, ou_ref, od_ref,
    qbuf, vbuf, rates, ke, kbuf, sbuf, rbuf, gbuf, wg, state, wlow, osl, win, oin,
    load, feed_s, feed_r, rs_s, rs_r, ag_s, ag_r, fw_s, fw_r, in_s, in_r, if_s, if_r, w_s, w_r, o_s, o_r,
):
    chips = rows_y * rows_x
    g = lax.axis_index("group")
    tok = lax.axis_index("tok")
    core = lax.rem(tok, 2)
    chip = tok // 2
    py, px = chip // rows_x, lax.rem(chip, rows_x)
    sib = chip * 2 + (1 - core)
    tokens, width = ke.shape[1], ke.shape[2]
    hid = state.shape[1]
    half = hid // 2
    per = width * half // 128 // chips
    share = wg.shape[2]

    def ring(d, n):
        return min(d, n - d)

    offsets = [(dy, dx) for dy in range(rows_y) for dx in range(rows_x) if (dy, dx) != (0, 0)]
    offsets.sort(key=lambda o: -(ring(o[0], rows_y) + ring(o[1], rows_x)))
    count = len(offsets)

    def ahead(n):
        dy, dx = offsets[n]
        return lax.rem(py + dy, rows_y) * rows_x + lax.rem(px + dx, rows_x)

    def behind(n):
        dy, dx = offsets[n]
        return lax.rem(py + (rows_y - dy), rows_y) * rows_x + lax.rem(px + (rows_x - dx), rows_x)

    def copy(src, dst, send, recv, where):
        return pltpu.make_async_remote_copy(
            src_ref=src, dst_ref=dst, send_sem=send, recv_sem=recv, device_id=where, device_id_type=MESH
        )

    loads = [
        pltpu.make_async_copy(v_ref.at[0], vbuf, load.at[0]),
        pltpu.make_async_copy(r_ref, rates, load.at[1]),
        pltpu.make_async_copy(k_ref.at[0], ke.at[0], load.at[2]),
        pltpu.make_async_copy(q_ref.at[0], qbuf, load.at[3]),
    ]
    barrier = pltpu.get_barrier_semaphore()

    def scale_values():
        for n in range(3):
            loads[n].wait()
        rate = jnp.broadcast_to(rates[...].astype(f32), (width, tokens)).T
        ke[1] = (-(rate * vbuf[...].astype(f32))).astype(bf16)

    def query(weights):
        pre = dot(qbuf[...], weights[0], NT)
        up = dot(qbuf[...], weights[1], NT)
        hidden = (pre * (0.5 + 0.5 * jnp.tanh(0.5 * pre)) * up).astype(bf16)
        oq_ref[0] = dot(hidden, weights[2]).astype(bf16)

    @pl.when(g > 0)
    def _():
        pl.semaphore_signal(barrier, inc=1, device_id=(0, tok), device_id_type=MESH)
        for n in range(4):
            loads[n].start()
        scale_values()
        pl.semaphore_wait(barrier, 1)
        feed = copy(ke, kbuf.at[g, core], feed_s, feed_r.at[g, core], (0, tok))
        feed.start()
        loads[3].wait()
        copy(wlow, win, w_s, w_r, (0, tok)).wait_recv()
        query([win[m] for m in range(3)])
        copy(osl, oin, o_s, o_r, (0, tok)).wait_recv()
        og_ref[0] = oin[0]
        ou_ref[0] = oin[1]
        od_ref[0] = oin[2]
        feed.wait_send()

    @pl.when(g == 0)
    def _():
        firsts = [
            pltpu.make_async_copy(ref, wg.at[tok, m], load.at[4 + m])
            for m, ref in enumerate((gi_ref, ui_ref, di_ref))
        ]
        for c in firsts:
            c.start()
        for n in range(4):
            loads[n].start()
        for n in range(count):
            pl.semaphore_signal(barrier, inc=1, device_id=(0, ahead(n) * 2 + core), device_id_type=MESH)
        pl.semaphore_signal(barrier, inc=1, device_id=(0, sib), device_id_type=MESH)
        for z in range(1, groups):
            pl.semaphore_signal(barrier, inc=1, device_id=(z, tok), device_id_type=MESH)
        for c in firsts:
            c.wait()
        pl.semaphore_wait(barrier, count + groups)

        def first_copy(n):
            return copy(wg.at[tok], wg.at[tok], in_s.at[n], in_r.at[n], (0, ahead(n) * 2 + core))

        def first_pass(n):
            slot = tok if n == count else behind(n) * 2 + core
            return copy(wg.at[slot], wg.at[slot], if_s.at[n], if_r.at[n], (0, sib))

        for n in range(count):
            first_copy(n).start()
        first_pass(count).start()
        scale_values()
        kbuf[0, core] = ke[...]
        feed = copy(ke, kbuf.at[0, core], feed_s, feed_r.at[0, core], (0, sib))
        feed.start()
        loads[3].wait()
        for n in reversed(range(count)):
            first_copy(n).wait_recv()
            first_pass(n).start()
        for n in reversed(range(count + 1)):
            first_pass(n).wait_recv()
        state[0] = wg[:, 0].reshape(width, hid).T
        state[1] = wg[:, 1].reshape(width, hid).T
        state[2] = wg[:, 2].reshape(hid, width)
        wlow[...] = state[...].astype(bf16)
        for n in range(count):
            first_copy(n).wait_send()
        for n in range(count + 1):
            first_pass(n).wait_send()
        feed.wait_send()

        def pick_outgoing():
            rows = lax.broadcasted_iota(jnp.int32, (16, width), 0)
            lanes = lax.broadcasted_iota(jnp.int32, (16, width), 1)
            for part in range(0, share, 16):
                size = min(16, share - part)
                one = jnp.where(lanes == rows + (tok * share + part), 1.0, 0.0).astype(bf16)
                for m in range(2):
                    full = state[m]
                    high, rest = split(full)
                    mid, low = split(full - high.astype(f32))
                    picked = dot(one, high, NT) + (dot(one, mid, NT) + dot(one, low, NT))
                    osl[m, part : part + size, :] = picked[:size]
            osl[2] = state[2, pl.ds(pl.multiple_of(tok * share, share), share), :]

        def slice_copy(n):
            return copy(
                sbuf.at[ahead(n)], rbuf.at[n], rs_s.at[n], rs_r.at[n], (0, ahead(n) * 2 + core)
            )

        def sum_copy(par, n):
            slot = gbuf.at[par, core, chip]
            return copy(slot, slot, ag_s.at[n], ag_r.at[n], (0, ahead(n) * 2 + core))

        def pass_copy(par, n):
            slot = gbuf.at[par, core, chip if n == count else behind(n)]
            return copy(slot, slot, fw_s.at[n], fw_r.at[par, n], (0, sib))

        def sums_sent(par):
            for n in range(count):
                sum_copy(par, n).wait_send()
            for n in range(count + 1):
                pass_copy(par, n).wait_send()

        def step(i, carry):
            par = lax.rem(i, 2)
            copy(ke, kbuf.at[i, 1 - core], feed_s, feed_r.at[i, 1 - core], (0, sib)).wait_recv()
            keys = kbuf[i, :, 0].reshape(2 * tokens, width)
            errs = kbuf[i, :, 1].reshape(2 * tokens, width)
            mine = pl.ds(pl.multiple_of(core * half, half), half)
            pre = dot(wlow[0, mine, :], keys, NT)
            up = dot(wlow[1, mine, :], keys, NT)
            back = dot(wlow[2, mine, :], errs, NT)
            sig = 0.5 + 0.5 * jnp.tanh(0.5 * pre)
            act = pre * sig
            slope = sig + act * (1.0 - sig)
            act_low = (act * up).astype(bf16)
            gate_diff = (back * up * slope).astype(bf16)
            up_diff = (back * act).astype(bf16)
            partial = (dot(gate_diff, keys), dot(up_diff, keys), dot(act_low, errs))
            for m in range(3):
                low = partial[m].astype(bf16)
                for s in range(width // 128):
                    span = chips * 128 // width
                    sbuf[s * span : (s + 1) * span, m] = low[:, s * 128 : (s + 1) * 128].reshape(
                        span, per, 128
                    )
            for n in range(count):
                slice_copy(n).start()

            weights_out = copy(wlow, win, w_s, w_r, (i, tok))
            slices_out = copy(osl, oin, o_s, o_r, (i - 1, tok))

            @pl.when(i == 0)
            def _():
                query([wlow[m] for m in range(3)])

            @pl.when(i > 0)
            def _():
                weights_out.start()
                pick_outgoing()
                sums_sent(1 - par)

            @pl.when(i == 1)
            def _():
                og_ref[0] = osl[0]
                ou_ref[0] = osl[1]
                od_ref[0] = osl[2]

            @pl.when(i > 1)
            def _():
                slices_out.start()

            for n in reversed(range(count)):
                slice_copy(n).wait_recv()
            total = sbuf[chip].astype(f32)
            for n in range(count):
                total = total + rbuf[n].astype(f32)
            gbuf[par, core, chip] = total.astype(bf16)

            for n in range(count):
                sum_copy(par, n).start()
            pass_copy(par, count).start()
            for n in range(count):
                slice_copy(n).wait_send()
            for n in reversed(range(count)):
                sum_copy(par, n).wait_recv()
                pass_copy(par, n).start()
            for n in reversed(range(count + 1)):
                pass_copy(par, n).wait_recv()

            coming = jnp.minimum(i + 1, groups - 1)
            pass_feed = copy(
                kbuf.at[coming, core], kbuf.at[coming, core], feed_s, feed_r.at[coming, core], (0, sib)
            )

            @pl.when(i < groups - 1)
            def _():
                pass_feed.wait_recv()
                pass_feed.start()

            grads = []
            for m in range(3):
                sides = []
                for c in range(2):
                    span = chips * 128 // width
                    sides.append(
                        jnp.concatenate(
                            [
                                gbuf[par, c, s * span : (s + 1) * span, m].reshape(half, 128)
                                for s in range(width // 128)
                            ],
                            axis=1,
                        )
                    )
                grads.append(jnp.concatenate(sides, axis=0).astype(f32))
            ortho = orthogonalize(grads)

            @pl.when(i < groups - 1)
            def _():
                pass_feed.wait_send()

            @pl.when(i > 0)
            def _():
                weights_out.wait_send()

            @pl.when(i > 1)
            def _():
                slices_out.wait_send()

            for m in range(3):
                before = state[m]
                stepped = before - UPDATE_SCALE * ortho[m]
                axis = 0 if m == 2 else 1
                target = jnp.sum(before * before, axis=axis, keepdims=True)
                present = jnp.sum(stepped * stepped, axis=axis, keepdims=True)
                after = stepped * (jnp.sqrt(target) * lax.rsqrt(present + 1e-06))
                state[m] = after
                wlow[m] = after.astype(bf16)
            return carry

        lax.fori_loop(0, groups, step, 0)
        pick_outgoing()
        last = copy(osl, oin, o_s, o_r, (groups - 1, tok))
        last.start()
        sums_sent((groups - 1) % 2)
        last.wait_send()


def solution(mesh):
    groups, devices = mesh.shape["group"], mesh.shape["tok"]
    chips = devices // 2
    rows_y = 4 if chips == 16 else 2
    rows_x = chips // rows_y

    def body(*args):
        _, key_rows, _, _, gate_init, _, down_init = args
        tokens, width = key_rows.shape[1:]
        share, hid = gate_init.shape
        share_w = down_init.shape[0]
        per = width * (hid // 2) // 128 // chips
        count = chips - 1
        vmem = pl.BlockSpec(memory_space=pltpu.VMEM)
        dma = pltpu.SemaphoreType.DMA
        return pl.pallas_call(
            functools.partial(kernel, groups, rows_y, rows_x),
            out_shape=(
                jax.ShapeDtypeStruct((1, tokens, width), bf16),
                jax.ShapeDtypeStruct((1, share, hid), f32),
                jax.ShapeDtypeStruct((1, share, hid), f32),
                jax.ShapeDtypeStruct((1, share_w, width), f32),
            ),
            in_specs=[pl.BlockSpec(memory_space=pltpu.MemorySpace.HBM)] * 7,
            out_specs=(vmem,) * 4,
            scratch_shapes=[
                pltpu.VMEM((tokens, width), bf16),
                pltpu.VMEM((tokens, width), bf16),
                pltpu.VMEM((1, tokens), bf16),
                pltpu.VMEM((2, tokens, width), bf16),
                pltpu.VMEM((groups, 2, 2, tokens, width), bf16),
                pltpu.VMEM((chips, 3, per, 128), bf16),
                pltpu.VMEM((count, 3, per, 128), bf16),
                pltpu.VMEM((2, 2, chips, 3, per, 128), bf16),
                pltpu.VMEM((devices, 3, share, hid), f32),
                pltpu.VMEM((3, hid, width), f32),
                pltpu.VMEM((3, hid, width), bf16),
                pltpu.VMEM((3, share, hid), f32),
                pltpu.VMEM((3, hid, width), bf16),
                pltpu.VMEM((3, share, hid), f32),
                dma((7,)),
                dma,
                dma((groups, 2)),
                dma((count,)),
                dma((count,)),
                dma((count,)),
                dma((count,)),
                dma((chips,)),
                dma((2, chips)),
                dma((count,)),
                dma((count,)),
                dma((chips,)),
                dma((chips,)),
                dma,
                dma,
                dma,
                dma,
            ],
            compiler_params=pltpu.CompilerParams(
                collective_id=0, has_side_effects=True, vmem_limit_bytes=48 * 1024 * 1024
            ),
            cost_estimate=pl.CostEstimate(flops=10**10, bytes_accessed=10**7, transcendentals=10**6),
        )(*[pltpu.with_memory_space_constraint(x, pltpu.MemorySpace.HBM) for x in args])

    rows = P("group", "tok", None)
    return jax.shard_map(
        body,
        mesh=mesh,
        in_specs=(rows, rows, rows, P("group", "tok"), P("tok", None), P("tok", None), P("tok", None)),
        out_specs=(rows, rows, rows, rows),
        check_vma=False,
    )
```

```python
import functools

import jax
import jax.numpy as jnp
from jax import lax
from jax.experimental import pallas as pl
from jax.experimental.pallas import tpu as pltpu
from jax.sharding import PartitionSpec as P

MESH = pl.DeviceIdType.MESH
NS_STEPS = 3
COEFF_A, COEFF_B, COEFF_C = (3.4445, -4.775, 2.0315)
UPDATE_SCALE = 0.5
f32, bf16 = jnp.float32, jnp.bfloat16
NN = (((1,), (0,)), ((), ()))
NT = (((1,), (1,)), ((), ()))


def dot(a, b, dims=NN):
    return lax.dot_general(a, b, dims, preferred_element_type=f32)


def split(a):
    high = a.astype(bf16)
    return high, (a - high.astype(f32)).astype(bf16)


def orthogonalize(grads):
    states = [g * lax.rsqrt(jnp.sum(g * g) + 1e-06) for g in grads]
    for repeat in range(NS_STEPS):
        highs = [x.astype(bf16) for x in states]
        grams = [dot(h, h, NT) for h in highs]
        lows = [m.astype(bf16) for m in grams]
        squares = [dot(m, m) for m in lows]
        polys = [COEFF_B * m + COEFF_C * s for m, s in zip(grams, squares)]
        if repeat + 1 < NS_STEPS:
            moves = [dot(p.astype(bf16), h) for p, h in zip(polys, highs)]
        else:
            moves = []
            for p, x in zip(polys, states):
                (ph, pl_), (xh, xl) = split(p), split(x)
                moves.append(dot(ph, xh) + (dot(ph, xl) + dot(pl_, xh)))
        states = [COEFF_A * x + m for x, m in zip(states, moves)]
    return states


def kernel(
    groups, rows_y, rows_x,
    q_ref, k_ref, v_ref, r_ref, gi_ref, ui_ref, di_ref,
    oq_ref, og_ref, ou_ref, od_ref,
    qbuf, vbuf, rates, ke, kbuf, sbuf, rbuf, gbuf, wg, state, wlow, osl, win, oin,
    load, feed_s, feed_r, rs_s, rs_r, ag_s, ag_r, fw_s, fw_r, in_s, in_r, if_s, if_r, w_s, w_r, o_s, o_r,
):
    chips = rows_y * rows_x
    g = lax.axis_index("group")
    tok = lax.axis_index("tok")
    core = lax.rem(tok, 2)
    chip = tok // 2
    py, px = chip // rows_x, lax.rem(chip, rows_x)
    sib = chip * 2 + (1 - core)
    tokens, width = ke.shape[1], ke.shape[2]
    hid = state.shape[1]
    half = hid // 2
    per = width * half // 128 // chips
    share = wg.shape[2]

    def ring(d, n):
        return min(d, n - d)

    offsets = [(dy, dx) for dy in range(rows_y) for dx in range(rows_x) if (dy, dx) != (0, 0)]
    offsets.sort(key=lambda o: -(ring(o[0], rows_y) + ring(o[1], rows_x)))
    count = len(offsets)

    def ahead(n):
        dy, dx = offsets[n]
        return lax.rem(py + dy, rows_y) * rows_x + lax.rem(px + dx, rows_x)

    def behind(n):
        dy, dx = offsets[n]
        return lax.rem(py + (rows_y - dy), rows_y) * rows_x + lax.rem(px + (rows_x - dx), rows_x)

    def copy(src, dst, send, recv, where):
        return pltpu.make_async_remote_copy(
            src_ref=src, dst_ref=dst, send_sem=send, recv_sem=recv, device_id=where, device_id_type=MESH
        )

    loads = [
        pltpu.make_async_copy(v_ref.at[0], vbuf, load.at[0]),
        pltpu.make_async_copy(r_ref, rates, load.at[1]),
        pltpu.make_async_copy(k_ref.at[0], ke.at[0], load.at[2]),
        pltpu.make_async_copy(q_ref.at[0], qbuf, load.at[3]),
    ]
    barrier = pltpu.get_barrier_semaphore()

    def scale_values():
        for n in range(3):
            loads[n].wait()
        rate = jnp.broadcast_to(rates[...].astype(f32), (width, tokens)).T
        ke[1] = (-(rate * vbuf[...].astype(f32))).astype(bf16)

    def query(weights):
        pre = dot(qbuf[...], weights[0], NT)
        up = dot(qbuf[...], weights[1], NT)
        hidden = (pre * (0.5 + 0.5 * jnp.tanh(0.5 * pre)) * up).astype(bf16)
        oq_ref[0] = dot(hidden, weights[2]).astype(bf16)

    @pl.when(g > 0)
    def _():
        for n in range(4):
            loads[n].start()
        scale_values()
        pl.semaphore_wait(barrier, 1)
        feed = copy(ke, kbuf.at[g, core], feed_s, feed_r.at[g, core], (0, tok))
        feed.start()
        loads[3].wait()
        copy(wlow, win, w_s, w_r, (0, tok)).wait_recv()
        query([win[m] for m in range(3)])
        copy(osl, oin, o_s, o_r, (0, tok)).wait_recv()
        og_ref[0] = oin[0]
        ou_ref[0] = oin[1]
        od_ref[0] = oin[2]
        feed.wait_send()

    @pl.when(g == 0)
    def _():
        for z in range(1, groups):
            pl.semaphore_signal(barrier, inc=1, device_id=(z, tok), device_id_type=MESH)
        firsts = [
            pltpu.make_async_copy(ref, wg.at[tok, m], load.at[4 + m])
            for m, ref in enumerate((gi_ref, ui_ref, di_ref))
        ]
        for c in firsts:
            c.start()
        for n in range(4):
            loads[n].start()
        for n in range(count):
            pl.semaphore_signal(barrier, inc=1, device_id=(0, ahead(n) * 2 + core), device_id_type=MESH)
        pl.semaphore_signal(barrier, inc=1, device_id=(0, sib), device_id_type=MESH)
        for c in firsts:
            c.wait()
        pl.semaphore_wait(barrier, count + 1)

        def first_copy(n):
            return copy(wg.at[tok], wg.at[tok], in_s.at[n], in_r.at[n], (0, ahead(n) * 2 + core))

        def first_pass(n):
            slot = tok if n == count else behind(n) * 2 + core
            return copy(wg.at[slot], wg.at[slot], if_s.at[n], if_r.at[n], (0, sib))

        for n in range(count):
            first_copy(n).start()
        first_pass(count).start()
        scale_values()
        kbuf[0, core] = ke[...]
        feed = copy(ke, kbuf.at[0, core], feed_s, feed_r.at[0, core], (0, sib))
        feed.start()
        loads[3].wait()
        for n in reversed(range(count)):
            first_copy(n).wait_recv()
            first_pass(n).start()
        for n in reversed(range(count + 1)):
            first_pass(n).wait_recv()
        state[0] = wg[:, 0].reshape(width, hid).T
        state[1] = wg[:, 1].reshape(width, hid).T
        state[2] = wg[:, 2].reshape(hid, width)
        wlow[...] = state[...].astype(bf16)
        for n in range(count):
            first_copy(n).wait_send()
        for n in range(count + 1):
            first_pass(n).wait_send()
        feed.wait_send()

        def pick_outgoing():
            rows = lax.broadcasted_iota(jnp.int32, (16, width), 0)
            lanes = lax.broadcasted_iota(jnp.int32, (16, width), 1)
            for part in range(0, share, 16):
                size = min(16, share - part)
                one = jnp.where(lanes == rows + (tok * share + part), 1.0, 0.0).astype(bf16)
                for m in range(2):
                    full = state[m]
                    high, rest = split(full)
                    mid, low = split(full - high.astype(f32))
                    picked = dot(one, high, NT) + (dot(one, mid, NT) + dot(one, low, NT))
                    osl[m, part : part + size, :] = picked[:size]
            osl[2] = state[2, pl.ds(pl.multiple_of(tok * share, share), share), :]

        def slice_copy(n):
            return copy(
                sbuf.at[ahead(n)], rbuf.at[n], rs_s.at[n], rs_r.at[n], (0, ahead(n) * 2 + core)
            )

        def sum_copy(par, n):
            slot = gbuf.at[par, core, chip]
            return copy(slot, slot, ag_s.at[n], ag_r.at[n], (0, ahead(n) * 2 + core))

        def pass_copy(par, n):
            slot = gbuf.at[par, core, chip if n == count else behind(n)]
            return copy(slot, slot, fw_s.at[n], fw_r.at[par, n], (0, sib))

        def sums_sent(par):
            for n in range(count):
                sum_copy(par, n).wait_send()
            for n in range(count + 1):
                pass_copy(par, n).wait_send()

        def step(i, carry):
            par = lax.rem(i, 2)
            copy(ke, kbuf.at[i, 1 - core], feed_s, feed_r.at[i, 1 - core], (0, sib)).wait_recv()
            keys = kbuf[i, :, 0].reshape(2 * tokens, width)
            errs = kbuf[i, :, 1].reshape(2 * tokens, width)
            mine = pl.ds(pl.multiple_of(core * half, half), half)
            pre = dot(wlow[0, mine, :], keys, NT)
            up = dot(wlow[1, mine, :], keys, NT)
            back = dot(wlow[2, mine, :], errs, NT)
            sig = 0.5 + 0.5 * jnp.tanh(0.5 * pre)
            act = pre * sig
            slope = sig + act * (1.0 - sig)
            act_low = (act * up).astype(bf16)
            gate_diff = (back * up * slope).astype(bf16)
            up_diff = (back * act).astype(bf16)
            partial = (dot(gate_diff, keys), dot(up_diff, keys), dot(act_low, errs))
            for m in range(3):
                low = partial[m].astype(bf16)
                for s in range(width // 128):
                    span = chips * 128 // width
                    sbuf[s * span : (s + 1) * span, m] = low[:, s * 128 : (s + 1) * 128].reshape(
                        span, per, 128
                    )
            for n in range(count):
                slice_copy(n).start()

            weights_out = copy(wlow, win, w_s, w_r, (i, tok))
            slices_out = copy(osl, oin, o_s, o_r, (i - 1, tok))

            @pl.when(i == 0)
            def _():
                query([wlow[m] for m in range(3)])

            @pl.when(i > 0)
            def _():
                weights_out.start()
                pick_outgoing()
                sums_sent(1 - par)

            @pl.when(i == 1)
            def _():
                og_ref[0] = osl[0]
                ou_ref[0] = osl[1]
                od_ref[0] = osl[2]

            @pl.when(i > 1)
            def _():
                slices_out.start()

            for n in reversed(range(count)):
                slice_copy(n).wait_recv()
            total = sbuf[chip].astype(f32)
            for n in range(count):
                total = total + rbuf[n].astype(f32)
            gbuf[par, core, chip] = total.astype(bf16)

            for n in range(count):
                sum_copy(par, n).start()
            pass_copy(par, count).start()
            for n in range(count):
                slice_copy(n).wait_send()
            for n in reversed(range(count)):
                sum_copy(par, n).wait_recv()
                pass_copy(par, n).start()
            for n in reversed(range(count + 1)):
                pass_copy(par, n).wait_recv()

            coming = jnp.minimum(i + 1, groups - 1)
            pass_feed = copy(
                kbuf.at[coming, core], kbuf.at[coming, core], feed_s, feed_r.at[coming, core], (0, sib)
            )

            @pl.when(i < groups - 1)
            def _():
                pass_feed.wait_recv()
                pass_feed.start()

            grads = []
            for m in range(3):
                sides = []
                for c in range(2):
                    span = chips * 128 // width
                    sides.append(
                        jnp.concatenate(
                            [
                                gbuf[par, c, s * span : (s + 1) * span, m].reshape(half, 128)
                                for s in range(width // 128)
                            ],
                            axis=1,
                        )
                    )
                grads.append(jnp.concatenate(sides, axis=0).astype(f32))
            ortho = orthogonalize(grads)

            @pl.when(i < groups - 1)
            def _():
                pass_feed.wait_send()

            @pl.when(i > 0)
            def _():
                weights_out.wait_send()

            @pl.when(i > 1)
            def _():
                slices_out.wait_send()

            for m in range(3):
                before = state[m]
                stepped = before - UPDATE_SCALE * ortho[m]
                axis = 0 if m == 2 else 1
                target = jnp.sum(before * before, axis=axis, keepdims=True)
                present = jnp.sum(stepped * stepped, axis=axis, keepdims=True)
                after = stepped * (jnp.sqrt(target) * lax.rsqrt(present + 1e-06))
                state[m] = after
                wlow[m] = after.astype(bf16)
            return carry

        lax.fori_loop(0, groups, step, 0)
        pick_outgoing()
        last = copy(osl, oin, o_s, o_r, (groups - 1, tok))
        last.start()
        sums_sent((groups - 1) % 2)
        last.wait_send()


def solution(mesh):
    groups, devices = mesh.shape["group"], mesh.shape["tok"]
    chips = devices // 2
    rows_y = 4 if chips == 16 else 2
    rows_x = chips // rows_y

    def body(*args):
        _, key_rows, _, _, gate_init, _, down_init = args
        tokens, width = key_rows.shape[1:]
        share, hid = gate_init.shape
        share_w = down_init.shape[0]
        per = width * (hid // 2) // 128 // chips
        count = chips - 1
        vmem = pl.BlockSpec(memory_space=pltpu.VMEM)
        dma = pltpu.SemaphoreType.DMA
        return pl.pallas_call(
            functools.partial(kernel, groups, rows_y, rows_x),
            out_shape=(
                jax.ShapeDtypeStruct((1, tokens, width), bf16),
                jax.ShapeDtypeStruct((1, share, hid), f32),
                jax.ShapeDtypeStruct((1, share, hid), f32),
                jax.ShapeDtypeStruct((1, share_w, width), f32),
            ),
            in_specs=[pl.BlockSpec(memory_space=pltpu.MemorySpace.HBM)] * 7,
            out_specs=(vmem,) * 4,
            scratch_shapes=[
                pltpu.VMEM((tokens, width), bf16),
                pltpu.VMEM((tokens, width), bf16),
                pltpu.VMEM((1, tokens), bf16),
                pltpu.VMEM((2, tokens, width), bf16),
                pltpu.VMEM((groups, 2, 2, tokens, width), bf16),
                pltpu.VMEM((chips, 3, per, 128), bf16),
                pltpu.VMEM((count, 3, per, 128), bf16),
                pltpu.VMEM((2, 2, chips, 3, per, 128), bf16),
                pltpu.VMEM((devices, 3, share, hid), f32),
                pltpu.VMEM((3, hid, width), f32),
                pltpu.VMEM((3, hid, width), bf16),
                pltpu.VMEM((3, share, hid), f32),
                pltpu.VMEM((3, hid, width), bf16),
                pltpu.VMEM((3, share, hid), f32),
                dma((7,)),
                dma,
                dma((groups, 2)),
                dma((count,)),
                dma((count,)),
                dma((count,)),
                dma((count,)),
                dma((chips,)),
                dma((2, chips)),
                dma((count,)),
                dma((count,)),
                dma((chips,)),
                dma((chips,)),
                dma,
                dma,
                dma,
                dma,
            ],
            compiler_params=pltpu.CompilerParams(
                collective_id=0, has_side_effects=True, vmem_limit_bytes=48 * 1024 * 1024
            ),
            cost_estimate=pl.CostEstimate(flops=10**10, bytes_accessed=10**7, transcendentals=10**6),
        )(*[pltpu.with_memory_space_constraint(x, pltpu.MemorySpace.HBM) for x in args])

    rows = P("group", "tok", None)
    return jax.shard_map(
        body,
        mesh=mesh,
        in_specs=(rows, rows, rows, P("group", "tok"), P("tok", None), P("tok", None), P("tok", None)),
        out_specs=(rows, rows, rows, rows),
        check_vma=False,
    )
```

```python
import functools

import jax
import jax.numpy as jnp
from jax import lax
from jax.experimental import pallas as pl
from jax.experimental.pallas import tpu as pltpu
from jax.sharding import PartitionSpec as P

MESH = pl.DeviceIdType.MESH
NS_STEPS = 3
COEFF_A, COEFF_B, COEFF_C = (3.4445, -4.775, 2.0315)
UPDATE_SCALE = 0.5
f32, bf16 = jnp.float32, jnp.bfloat16
NN = (((1,), (0,)), ((), ()))
NT = (((1,), (1,)), ((), ()))


def dot(a, b, dims=NN):
    return lax.dot_general(a, b, dims, preferred_element_type=f32)


def split(a):
    high = a.astype(bf16)
    return high, (a - high.astype(f32)).astype(bf16)


def orthogonalize(grads):
    wide = [g.astype(f32) for g in grads]
    scales = [lax.rsqrt(jnp.sum(g * g) + 1e-06) for g in wide]
    states = None
    for repeat in range(NS_STEPS):
        if repeat == 0:
            highs = grads
            grams = [(s * s) * dot(h, h, NT) for h, s in zip(highs, scales)]
        else:
            highs = [x.astype(bf16) for x in states]
            grams = [dot(h, h, NT) for h in highs]
        lows = [m.astype(bf16) for m in grams]
        squares = [dot(m, m) for m in lows]
        polys = [COEFF_B * m + COEFF_C * s for m, s in zip(grams, squares)]
        if repeat == 0:
            moves = [dot(p.astype(bf16), h) for p, h in zip(polys, highs)]
            states = [s * (COEFF_A * x + m) for s, x, m in zip(scales, wide, moves)]
        elif repeat + 1 < NS_STEPS:
            moves = [dot(p.astype(bf16), h) for p, h in zip(polys, highs)]
            states = [COEFF_A * x + m for x, m in zip(states, moves)]
        else:
            moves = []
            for p, x in zip(polys, states):
                (ph, pl_), (xh, xl) = split(p), split(x)
                moves.append(dot(ph, xh) + (dot(ph, xl) + dot(pl_, xh)))
            states = [COEFF_A * x + m for x, m in zip(states, moves)]
    return states


def kernel(
    groups, rows_y, rows_x,
    q_ref, k_ref, v_ref, r_ref, gi_ref, ui_ref, di_ref,
    oq_ref, rows_ref,
    qbuf, vbuf, rates, ke, kbuf, sbuf, rbuf, gbuf, wg, state, wlow, osl, win, oin,
    load, feed_s, feed_r, rs_s, rs_r, ag_s, ag_r, fw_s, fw_r, in_s, in_r, if_s, if_r, w_s, w_r, o_s, o_r,
):
    chips = rows_y * rows_x
    g = lax.axis_index("group")
    tok = lax.axis_index("tok")
    core = lax.rem(tok, 2)
    chip = tok // 2
    py, px = chip // rows_x, lax.rem(chip, rows_x)
    sib = chip * 2 + (1 - core)
    tokens, width = ke.shape[1], ke.shape[2]
    hid = state.shape[1]
    half = hid // 2
    per = width * half // 128 // chips
    share = wg.shape[2]

    def ring(d, n):
        return min(d, n - d)

    offsets = [(dy, dx) for dy in range(rows_y) for dx in range(rows_x) if (dy, dx) != (0, 0)]
    offsets.sort(key=lambda o: -(ring(o[0], rows_y) + ring(o[1], rows_x)))
    count = len(offsets)

    def ahead(n):
        dy, dx = offsets[n]
        return lax.rem(py + dy, rows_y) * rows_x + lax.rem(px + dx, rows_x)

    def behind(n):
        dy, dx = offsets[n]
        return lax.rem(py + (rows_y - dy), rows_y) * rows_x + lax.rem(px + (rows_x - dx), rows_x)

    def copy(src, dst, send, recv, where):
        return pltpu.make_async_remote_copy(
            src_ref=src, dst_ref=dst, send_sem=send, recv_sem=recv, device_id=where, device_id_type=MESH
        )

    loads = [
        pltpu.make_async_copy(v_ref.at[0], vbuf, load.at[0]),
        pltpu.make_async_copy(r_ref, rates, load.at[1]),
        pltpu.make_async_copy(k_ref.at[0], ke.at[0], load.at[2]),
        pltpu.make_async_copy(q_ref.at[0], qbuf, load.at[3]),
    ]
    barrier = pltpu.get_barrier_semaphore()

    def scale_values():
        for n in range(3):
            loads[n].wait()
        rate = jnp.broadcast_to(rates[...].astype(f32), (width, tokens)).T
        ke[1] = (-(rate * vbuf[...].astype(f32))).astype(bf16)

    def query(weights):
        pre = dot(qbuf[...], weights[0], NT)
        up = dot(qbuf[...], weights[1], NT)
        hidden = (pre * (0.5 + 0.5 * jnp.tanh(0.5 * pre)) * up).astype(bf16)
        oq_ref[0] = dot(hidden, weights[2]).astype(bf16)

    @pl.when(g > 0)
    def _():
        for n in range(4):
            loads[n].start()
        scale_values()
        pl.semaphore_wait(barrier, 1)
        feed = copy(ke, kbuf.at[g, core], feed_s, feed_r.at[g, core], (0, tok))
        feed.start()
        loads[3].wait()
        copy(wlow, win, w_s, w_r, (0, tok)).wait_recv()
        query([win[m] for m in range(3)])
        copy(osl, oin, o_s, o_r, (0, tok)).wait_recv()
        rows_ref[...] = oin[...]
        feed.wait_send()

    @pl.when(g == 0)
    def _():
        for z in range(1, groups):
            pl.semaphore_signal(barrier, inc=1, device_id=(z, tok), device_id_type=MESH)
        firsts = [
            pltpu.make_async_copy(ref, wg.at[tok, m], load.at[4 + m])
            for m, ref in enumerate((gi_ref, ui_ref, di_ref))
        ]
        for c in firsts:
            c.start()
        for n in range(4):
            loads[n].start()
        for n in range(count):
            pl.semaphore_signal(barrier, inc=1, device_id=(0, ahead(n) * 2 + core), device_id_type=MESH)
        pl.semaphore_signal(barrier, inc=1, device_id=(0, sib), device_id_type=MESH)
        for c in firsts:
            c.wait()
        pl.semaphore_wait(barrier, count + 1)

        def first_copy(n):
            return copy(wg.at[tok], wg.at[tok], in_s.at[n], in_r.at[n], (0, ahead(n) * 2 + core))

        def first_pass(n):
            slot = tok if n == count else behind(n) * 2 + core
            return copy(wg.at[slot], wg.at[slot], if_s.at[n], if_r.at[n], (0, sib))

        for n in range(count):
            first_copy(n).start()
        first_pass(count).start()
        scale_values()
        kbuf[0, core] = ke[...]
        feed = copy(ke, kbuf.at[0, core], feed_s, feed_r.at[0, core], (0, sib))
        feed.start()
        loads[3].wait()
        for n in reversed(range(count)):
            first_copy(n).wait_recv()
            first_pass(n).start()
        for n in reversed(range(count + 1)):
            first_pass(n).wait_recv()
        state[0] = wg[:, 0].reshape(width, hid).T
        state[1] = wg[:, 1].reshape(width, hid).T
        state[2] = wg[:, 2].reshape(hid, width)
        wlow[...] = state[...].astype(bf16)
        for n in range(count):
            first_copy(n).wait_send()
        for n in range(count + 1):
            first_pass(n).wait_send()
        feed.wait_send()

        def pick_outgoing():
            rows = lax.broadcasted_iota(jnp.int32, (16, width), 0)
            lanes = lax.broadcasted_iota(jnp.int32, (16, width), 1)
            for part in range(0, share, 16):
                size = min(16, share - part)
                one = jnp.where(lanes == rows + (tok * share + part), 1.0, 0.0).astype(bf16)
                for m in range(2):
                    full = state[m]
                    high, rest = split(full)
                    mid, low = split(full - high.astype(f32))
                    picked = dot(one, high, NT) + (dot(one, mid, NT) + dot(one, low, NT))
                    osl[m, part : part + size, :] = picked[:size]
            osl[2] = state[2, pl.ds(pl.multiple_of(tok * share, share), share), :]

        def slice_copy(n):
            return copy(
                sbuf.at[ahead(n)], rbuf.at[n], rs_s.at[n], rs_r.at[n], (0, ahead(n) * 2 + core)
            )

        def sum_copy(par, n):
            slot = gbuf.at[par, core, chip]
            return copy(slot, slot, ag_s.at[n], ag_r.at[n], (0, ahead(n) * 2 + core))

        def pass_copy(par, n):
            slot = gbuf.at[par, core, chip if n == count else behind(n)]
            return copy(slot, slot, fw_s.at[n], fw_r.at[par, n], (0, sib))

        def sums_sent(par):
            for n in range(count):
                sum_copy(par, n).wait_send()
            for n in range(count + 1):
                pass_copy(par, n).wait_send()

        def step(i, carry):
            par = lax.rem(i, 2)
            copy(ke, kbuf.at[i, 1 - core], feed_s, feed_r.at[i, 1 - core], (0, sib)).wait_recv()
            keys = kbuf[i, :, 0].reshape(2 * tokens, width)
            errs = kbuf[i, :, 1].reshape(2 * tokens, width)
            mine = pl.ds(pl.multiple_of(core * half, half), half)
            pre = dot(wlow[0, mine, :], keys, NT)
            up = dot(wlow[1, mine, :], keys, NT)
            back = dot(wlow[2, mine, :], errs, NT)
            sig = 0.5 + 0.5 * jnp.tanh(0.5 * pre)
            act = pre * sig
            slope = sig + act * (1.0 - sig)
            act_low = (act * up).astype(bf16)
            gate_diff = (back * up * slope).astype(bf16)
            up_diff = (back * act).astype(bf16)
            partial = (dot(gate_diff, keys), dot(up_diff, keys), dot(act_low, errs))
            for m in range(3):
                low = partial[m].astype(bf16)
                for s in range(width // 128):
                    span = chips * 128 // width
                    sbuf[s * span : (s + 1) * span, m] = low[:, s * 128 : (s + 1) * 128].reshape(
                        span, per, 128
                    )
            for n in range(count):
                slice_copy(n).start()

            weights_out = copy(wlow, win, w_s, w_r, (i, tok))
            slices_out = copy(osl, oin, o_s, o_r, (i - 1, tok))

            @pl.when(i == 0)
            def _():
                query([wlow[m] for m in range(3)])

            @pl.when(i > 0)
            def _():
                weights_out.start()
                pick_outgoing()
                sums_sent(1 - par)

            @pl.when(i == 1)
            def _():
                rows_ref[...] = osl[...]

            @pl.when(i > 1)
            def _():
                slices_out.start()

            for n in reversed(range(count)):
                slice_copy(n).wait_recv()
            total = sbuf[chip].astype(f32)
            for n in range(count):
                total = total + rbuf[n].astype(f32)
            gbuf[par, core, chip] = total.astype(bf16)

            for n in range(count):
                sum_copy(par, n).start()
            pass_copy(par, count).start()
            for n in range(count):
                slice_copy(n).wait_send()
            for n in reversed(range(count)):
                sum_copy(par, n).wait_recv()
                pass_copy(par, n).start()
            for n in reversed(range(count + 1)):
                pass_copy(par, n).wait_recv()

            coming = jnp.minimum(i + 1, groups - 1)
            pass_feed = copy(
                kbuf.at[coming, core], kbuf.at[coming, core], feed_s, feed_r.at[coming, core], (0, sib)
            )

            @pl.when(i < groups - 1)
            def _():
                pass_feed.wait_recv()
                pass_feed.start()

            grads = []
            for m in range(3):
                sides = []
                for c in range(2):
                    span = chips * 128 // width
                    sides.append(
                        jnp.concatenate(
                            [
                                gbuf[par, c, s * span : (s + 1) * span, m].reshape(half, 128)
                                for s in range(width // 128)
                            ],
                            axis=1,
                        )
                    )
                grads.append(jnp.concatenate(sides, axis=0))
            ortho = orthogonalize(grads)

            @pl.when(i < groups - 1)
            def _():
                pass_feed.wait_send()

            @pl.when(i > 0)
            def _():
                weights_out.wait_send()

            @pl.when(i > 1)
            def _():
                slices_out.wait_send()

            for m in range(3):
                before = state[m]
                stepped = before - UPDATE_SCALE * ortho[m]
                axis = 0 if m == 2 else 1
                target = jnp.sum(before * before, axis=axis, keepdims=True)
                present = jnp.sum(stepped * stepped, axis=axis, keepdims=True)
                after = stepped * (jnp.sqrt(target) * lax.rsqrt(present + 1e-06))
                state[m] = after
                wlow[m] = after.astype(bf16)
            return carry

        lax.fori_loop(0, groups, step, 0)
        pick_outgoing()
        last = copy(osl, oin, o_s, o_r, (groups - 1, tok))
        last.start()
        sums_sent((groups - 1) % 2)
        last.wait_send()


def solution(mesh):
    groups, devices = mesh.shape["group"], mesh.shape["tok"]
    chips = devices // 2
    rows_y = 4 if chips == 16 else 2
    rows_x = chips // rows_y

    def body(*args):
        _, key_rows, _, _, gate_init, _, down_init = args
        tokens, width = key_rows.shape[1:]
        share, hid = gate_init.shape
        share_w = down_init.shape[0]
        per = width * (hid // 2) // 128 // chips
        count = chips - 1
        vmem = pl.BlockSpec(memory_space=pltpu.VMEM)
        dma = pltpu.SemaphoreType.DMA
        outputs, slices = pl.pallas_call(
            functools.partial(kernel, groups, rows_y, rows_x),
            out_shape=(
                jax.ShapeDtypeStruct((1, tokens, width), bf16),
                jax.ShapeDtypeStruct((3, share, hid), f32),
            ),
            in_specs=[pl.BlockSpec(memory_space=pltpu.MemorySpace.HBM)] * 7,
            out_specs=(vmem,) * 2,
            scratch_shapes=[
                pltpu.VMEM((tokens, width), bf16),
                pltpu.VMEM((tokens, width), bf16),
                pltpu.VMEM((1, tokens), bf16),
                pltpu.VMEM((2, tokens, width), bf16),
                pltpu.VMEM((groups, 2, 2, tokens, width), bf16),
                pltpu.VMEM((chips, 3, per, 128), bf16),
                pltpu.VMEM((count, 3, per, 128), bf16),
                pltpu.VMEM((2, 2, chips, 3, per, 128), bf16),
                pltpu.VMEM((devices, 3, share, hid), f32),
                pltpu.VMEM((3, hid, width), f32),
                pltpu.VMEM((3, hid, width), bf16),
                pltpu.VMEM((3, share, hid), f32),
                pltpu.VMEM((3, hid, width), bf16),
                pltpu.VMEM((3, share, hid), f32),
                dma((7,)),
                dma,
                dma((groups, 2)),
                dma((count,)),
                dma((count,)),
                dma((count,)),
                dma((count,)),
                dma((chips,)),
                dma((2, chips)),
                dma((count,)),
                dma((count,)),
                dma((chips,)),
                dma((chips,)),
                dma,
                dma,
                dma,
                dma,
            ],
            compiler_params=pltpu.CompilerParams(
                collective_id=0, has_side_effects=True, vmem_limit_bytes=48 * 1024 * 1024
            ),
            cost_estimate=pl.CostEstimate(flops=10**10, bytes_accessed=10**7, transcendentals=10**6),
        )(*[pltpu.with_memory_space_constraint(x, pltpu.MemorySpace.HBM) for x in args])
        return outputs, slices[0:1], slices[1:2], slices[2:3]

    rows = P("group", "tok", None)
    return jax.shard_map(
        body,
        mesh=mesh,
        in_specs=(rows, rows, rows, P("group", "tok"), P("tok", None), P("tok", None), P("tok", None)),
        out_specs=(rows, rows, rows, rows),
        check_vma=False,
    )
```

```python
import functools

import jax
import jax.numpy as jnp
from jax import lax
from jax.experimental import pallas as pl
from jax.experimental.pallas import tpu as pltpu
from jax.sharding import PartitionSpec as P

MESH = pl.DeviceIdType.MESH
NS_STEPS = 3
COEFF_A, COEFF_B, COEFF_C = (3.4445, -4.775, 2.0315)
UPDATE_SCALE = 0.5
f32, bf16 = jnp.float32, jnp.bfloat16
NN = (((1,), (0,)), ((), ()))
NT = (((1,), (1,)), ((), ()))


def dot(a, b, dims=NN):
    return lax.dot_general(a, b, dims, preferred_element_type=f32)


def split(a):
    high = a.astype(bf16)
    return high, (a - high.astype(f32)).astype(bf16)


def orthogonalize(grads):
    wide = [g.astype(f32) for g in grads]
    scales = [lax.rsqrt(jnp.sum(g * g) + 1e-06) for g in wide]
    states = None
    for repeat in range(NS_STEPS):
        if repeat == 0:
            highs = grads
            grams = [(s * s) * dot(h, h, NT) for h, s in zip(highs, scales)]
        else:
            highs = [x.astype(bf16) for x in states]
            grams = [dot(h, h, NT) for h in highs]
        lows = [m.astype(bf16) for m in grams]
        squares = [dot(m, m) for m in lows]
        polys = [COEFF_B * m + COEFF_C * s for m, s in zip(grams, squares)]
        if repeat == 0:
            moves = [dot(p.astype(bf16), h) for p, h in zip(polys, highs)]
            states = [s * (COEFF_A * x + m) for s, x, m in zip(scales, wide, moves)]
        elif repeat + 1 < NS_STEPS:
            moves = [dot(p.astype(bf16), h) for p, h in zip(polys, highs)]
            states = [COEFF_A * x + m for x, m in zip(states, moves)]
        else:
            moves = []
            for p, x in zip(polys, states):
                (ph, pl_), (xh, xl) = split(p), split(x)
                moves.append(dot(ph, xh) + (dot(ph, xl) + dot(pl_, xh)))
            states = [COEFF_A * x + m for x, m in zip(states, moves)]
    return states


def kernel(
    groups, rows_y, rows_x,
    q_ref, k_ref, v_ref, r_ref, gi_ref, ui_ref, di_ref,
    oq_ref, rows_ref,
    qbuf, vbuf, rates, ke, kbuf, sbuf, rbuf, gbuf, own, wg, state, wlow, osl, win, oin,
    load, feed_s, feed_r, rs_s, rs_r, ag_s, ag_r, fw_s, fw_r, in_s, in_r, if_s, if_r, w_s, w_r, o_s, o_r,
):
    chips = rows_y * rows_x
    g = lax.axis_index("group")
    tok = lax.axis_index("tok")
    core = lax.rem(tok, 2)
    chip = tok // 2
    py, px = chip // rows_x, lax.rem(chip, rows_x)
    sib = chip * 2 + (1 - core)
    tokens, width = ke.shape[1], ke.shape[2]
    hid = state.shape[1]
    half = hid // 2
    per = width * half // 128 // chips
    share = own.shape[1]

    def ring(d, n):
        return min(d, n - d)

    offsets = [(dy, dx) for dy in range(rows_y) for dx in range(rows_x) if (dy, dx) != (0, 0)]
    offsets.sort(key=lambda o: -(ring(o[0], rows_y) + ring(o[1], rows_x)))
    count = len(offsets)

    def ahead(n):
        dy, dx = offsets[n]
        return lax.rem(py + dy, rows_y) * rows_x + lax.rem(px + dx, rows_x)

    def behind(n):
        dy, dx = offsets[n]
        return lax.rem(py + (rows_y - dy), rows_y) * rows_x + lax.rem(px + (rows_x - dx), rows_x)

    def copy(src, dst, send, recv, where):
        return pltpu.make_async_remote_copy(
            src_ref=src, dst_ref=dst, send_sem=send, recv_sem=recv, device_id=where, device_id_type=MESH
        )

    loads = [
        pltpu.make_async_copy(v_ref.at[0], vbuf, load.at[0]),
        pltpu.make_async_copy(r_ref, rates, load.at[1]),
        pltpu.make_async_copy(k_ref.at[0], ke.at[0], load.at[2]),
        pltpu.make_async_copy(q_ref.at[0], qbuf, load.at[3]),
    ]
    barrier = pltpu.get_barrier_semaphore()

    def scale_values():
        for n in range(3):
            loads[n].wait()
        rate = jnp.broadcast_to(rates[...].astype(f32), (width, tokens)).T
        ke[1] = (-(rate * vbuf[...].astype(f32))).astype(bf16)

    def query(weights):
        pre = dot(qbuf[...], weights[0], NT)
        up = dot(qbuf[...], weights[1], NT)
        hidden = (pre * (0.5 + 0.5 * jnp.tanh(0.5 * pre)) * up).astype(bf16)
        oq_ref[0] = dot(hidden, weights[2]).astype(bf16)

    @pl.when(g > 0)
    def _():
        for n in range(4):
            loads[n].start()
        scale_values()
        pl.semaphore_wait(barrier, 1)
        feed = copy(ke, kbuf.at[g, core], feed_s, feed_r.at[g, core], (0, tok))
        feed.start()
        loads[3].wait()
        copy(wlow, win, w_s, w_r, (0, tok)).wait_recv()
        query([win[m] for m in range(3)])
        copy(osl, oin, o_s, o_r, (0, tok)).wait_recv()
        rows_ref[...] = oin[...]
        feed.wait_send()

    @pl.when(g == 0)
    def _():
        for z in range(1, groups):
            pl.semaphore_signal(barrier, inc=1, device_id=(z, tok), device_id_type=MESH)
        firsts = [
            pltpu.make_async_copy(ref, own.at[m], load.at[4 + m])
            for m, ref in enumerate((gi_ref, ui_ref, di_ref))
        ]
        for c in firsts:
            c.start()
        for n in range(4):
            loads[n].start()
        for n in range(count):
            pl.semaphore_signal(barrier, inc=1, device_id=(0, ahead(n) * 2 + core), device_id_type=MESH)
        pl.semaphore_signal(barrier, inc=1, device_id=(0, sib), device_id_type=MESH)
        for c in firsts:
            c.wait()
        for w, value in enumerate(split(own[...].reshape(3 * share, hid))):
            wg[tok, w] = value
        pl.semaphore_wait(barrier, count + 1)

        def first_copy(w, n):
            slot = wg.at[tok, w]
            return copy(slot, slot, in_s.at[w, n], in_r.at[w, n], (0, ahead(n) * 2 + core))

        def first_pass(w, n):
            slot = wg.at[tok if n == count else behind(n) * 2 + core, w]
            return copy(slot, slot, if_s.at[w, n], if_r.at[w, n], (0, sib))

        def first_parts(w):
            wide = wg[:, w].astype(f32)
            gate, up, down = (
                wide[:, m * share : (m + 1) * share].reshape(width, hid) for m in range(3)
            )
            return gate.T, up.T, down

        def first_sent(w):
            for n in range(count):
                first_copy(w, n).wait_send()
            for n in range(count + 1):
                first_pass(w, n).wait_send()

        for n in range(count):
            first_copy(0, n).start()
        first_pass(0, count).start()
        scale_values()
        kbuf[0, core] = ke[...]
        feed = copy(ke, kbuf.at[0, core], feed_s, feed_r.at[0, core], (0, sib))
        feed.start()
        loads[3].wait()
        for n in reversed(range(count)):
            first_copy(0, n).wait_recv()
            first_pass(0, n).start()
        for n in reversed(range(count + 1)):
            first_pass(0, n).wait_recv()
        for m, value in enumerate(first_parts(0)):
            state[m] = value
        wlow[...] = state[...].astype(bf16)
        feed.wait_send()

        def pick_outgoing():
            rows = lax.broadcasted_iota(jnp.int32, (16, width), 0)
            lanes = lax.broadcasted_iota(jnp.int32, (16, width), 1)
            for part in range(0, share, 16):
                size = min(16, share - part)
                one = jnp.where(lanes == rows + (tok * share + part), 1.0, 0.0).astype(bf16)
                for m in range(2):
                    full = state[m]
                    high, rest = split(full)
                    mid, low = split(full - high.astype(f32))
                    picked = dot(one, high, NT) + (dot(one, mid, NT) + dot(one, low, NT))
                    osl[m, part : part + size, :] = picked[:size]
            osl[2] = state[2, pl.ds(pl.multiple_of(tok * share, share), share), :]

        def slice_copy(n):
            return copy(
                sbuf.at[ahead(n)], rbuf.at[n], rs_s.at[n], rs_r.at[n], (0, ahead(n) * 2 + core)
            )

        def sum_copy(par, n):
            slot = gbuf.at[par, core, chip]
            return copy(slot, slot, ag_s.at[n], ag_r.at[n], (0, ahead(n) * 2 + core))

        def pass_copy(par, n):
            slot = gbuf.at[par, core, chip if n == count else behind(n)]
            return copy(slot, slot, fw_s.at[n], fw_r.at[par, n], (0, sib))

        def sums_sent(par):
            for n in range(count):
                sum_copy(par, n).wait_send()
            for n in range(count + 1):
                pass_copy(par, n).wait_send()

        def step(i, carry):
            par = lax.rem(i, 2)
            copy(ke, kbuf.at[i, 1 - core], feed_s, feed_r.at[i, 1 - core], (0, sib)).wait_recv()
            keys = kbuf[i, :, 0].reshape(2 * tokens, width)
            errs = kbuf[i, :, 1].reshape(2 * tokens, width)
            mine = pl.ds(pl.multiple_of(core * half, half), half)
            pre = dot(wlow[0, mine, :], keys, NT)
            up = dot(wlow[1, mine, :], keys, NT)
            back = dot(wlow[2, mine, :], errs, NT)
            sig = 0.5 + 0.5 * jnp.tanh(0.5 * pre)
            act = pre * sig
            slope = sig + act * (1.0 - sig)
            act_low = (act * up).astype(bf16)
            gate_diff = (back * up * slope).astype(bf16)
            up_diff = (back * act).astype(bf16)
            partial = (dot(gate_diff, keys), dot(up_diff, keys), dot(act_low, errs))
            for m in range(3):
                low = partial[m].astype(bf16)
                for s in range(width // 128):
                    span = chips * 128 // width
                    sbuf[s * span : (s + 1) * span, m] = low[:, s * 128 : (s + 1) * 128].reshape(
                        span, per, 128
                    )
            for n in range(count):
                slice_copy(n).start()

            weights_out = copy(wlow, win, w_s, w_r, (i, tok))
            slices_out = copy(osl, oin, o_s, o_r, (i - 1, tok))

            @pl.when(i == 0)
            def _():
                for n in range(count):
                    first_copy(1, n).start()
                first_pass(1, count).start()
                query([wlow[m] for m in range(3)])
                first_sent(0)

            @pl.when(i > 0)
            def _():
                weights_out.start()
                pick_outgoing()
                sums_sent(1 - par)

            @pl.when(i == 1)
            def _():
                rows_ref[...] = osl[...]

            @pl.when(i > 1)
            def _():
                slices_out.start()

            for n in reversed(range(count)):
                slice_copy(n).wait_recv()
            total = sbuf[chip].astype(f32)
            for n in range(count):
                total = total + rbuf[n].astype(f32)
            gbuf[par, core, chip] = total.astype(bf16)

            for n in range(count):
                sum_copy(par, n).start()
            pass_copy(par, count).start()
            for n in range(count):
                slice_copy(n).wait_send()
            for n in reversed(range(count)):
                sum_copy(par, n).wait_recv()
                pass_copy(par, n).start()
            for n in reversed(range(count + 1)):
                pass_copy(par, n).wait_recv()

            coming = jnp.minimum(i + 1, groups - 1)
            pass_feed = copy(
                kbuf.at[coming, core], kbuf.at[coming, core], feed_s, feed_r.at[coming, core], (0, sib)
            )

            @pl.when(i < groups - 1)
            def _():
                pass_feed.wait_recv()
                pass_feed.start()

            @pl.when(i == 0)
            def _():
                for n in reversed(range(count)):
                    first_copy(1, n).wait_recv()
                    first_pass(1, n).start()

            grads = []
            for m in range(3):
                sides = []
                for c in range(2):
                    span = chips * 128 // width
                    sides.append(
                        jnp.concatenate(
                            [
                                gbuf[par, c, s * span : (s + 1) * span, m].reshape(half, 128)
                                for s in range(width // 128)
                            ],
                            axis=1,
                        )
                    )
                grads.append(jnp.concatenate(sides, axis=0))
            ortho = orthogonalize(grads)

            @pl.when(i < groups - 1)
            def _():
                pass_feed.wait_send()

            @pl.when(i > 0)
            def _():
                weights_out.wait_send()

            @pl.when(i > 1)
            def _():
                slices_out.wait_send()

            @pl.when(i == 0)
            def _():
                for n in reversed(range(count + 1)):
                    first_pass(1, n).wait_recv()
                for m, value in enumerate(first_parts(1)):
                    state[m] = state[m] + value
                first_sent(1)

            for m in range(3):
                before = state[m]
                stepped = before - UPDATE_SCALE * ortho[m]
                axis = 0 if m == 2 else 1
                target = jnp.sum(before * before, axis=axis, keepdims=True)
                present = jnp.sum(stepped * stepped, axis=axis, keepdims=True)
                after = stepped * (jnp.sqrt(target) * lax.rsqrt(present + 1e-06))
                state[m] = after
                wlow[m] = after.astype(bf16)
            return carry

        lax.fori_loop(0, groups, step, 0)
        pick_outgoing()
        last = copy(osl, oin, o_s, o_r, (groups - 1, tok))
        last.start()
        sums_sent((groups - 1) % 2)
        last.wait_send()


def solution(mesh):
    groups, devices = mesh.shape["group"], mesh.shape["tok"]
    chips = devices // 2
    rows_y = 4 if chips == 16 else 2
    rows_x = chips // rows_y

    def body(*args):
        _, key_rows, _, _, gate_init, _, down_init = args
        tokens, width = key_rows.shape[1:]
        share, hid = gate_init.shape
        share_w = down_init.shape[0]
        per = width * (hid // 2) // 128 // chips
        count = chips - 1
        vmem = pl.BlockSpec(memory_space=pltpu.VMEM)
        dma = pltpu.SemaphoreType.DMA
        outputs, slices = pl.pallas_call(
            functools.partial(kernel, groups, rows_y, rows_x),
            out_shape=(
                jax.ShapeDtypeStruct((1, tokens, width), bf16),
                jax.ShapeDtypeStruct((3, share, hid), f32),
            ),
            in_specs=[pl.BlockSpec(memory_space=pltpu.MemorySpace.HBM)] * 7,
            out_specs=(vmem,) * 2,
            scratch_shapes=[
                pltpu.VMEM((tokens, width), bf16),
                pltpu.VMEM((tokens, width), bf16),
                pltpu.VMEM((1, tokens), bf16),
                pltpu.VMEM((2, tokens, width), bf16),
                pltpu.VMEM((groups, 2, 2, tokens, width), bf16),
                pltpu.VMEM((chips, 3, per, 128), bf16),
                pltpu.VMEM((count, 3, per, 128), bf16),
                pltpu.VMEM((2, 2, chips, 3, per, 128), bf16),
                pltpu.VMEM((3, share, hid), f32),
                pltpu.VMEM((devices, 2, 3 * share, hid), bf16),
                pltpu.VMEM((3, hid, width), f32),
                pltpu.VMEM((3, hid, width), bf16),
                pltpu.VMEM((3, share, hid), f32),
                pltpu.VMEM((3, hid, width), bf16),
                pltpu.VMEM((3, share, hid), f32),
                dma((7,)),
                dma,
                dma((groups, 2)),
                dma((count,)),
                dma((count,)),
                dma((count,)),
                dma((count,)),
                dma((chips,)),
                dma((2, chips)),
                dma((2, count)),
                dma((2, count)),
                dma((2, chips)),
                dma((2, chips)),
                dma,
                dma,
                dma,
                dma,
            ],
            compiler_params=pltpu.CompilerParams(
                collective_id=0, has_side_effects=True, vmem_limit_bytes=48 * 1024 * 1024
            ),
            cost_estimate=pl.CostEstimate(flops=10**10, bytes_accessed=10**7, transcendentals=10**6),
        )(*[pltpu.with_memory_space_constraint(x, pltpu.MemorySpace.HBM) for x in args])
        return outputs, slices[0:1], slices[1:2], slices[2:3]

    rows = P("group", "tok", None)
    return jax.shard_map(
        body,
        mesh=mesh,
        in_specs=(rows, rows, rows, P("group", "tok"), P("tok", None), P("tok", None), P("tok", None)),
        out_specs=(rows, rows, rows, rows),
        check_vma=False,
    )
```

```python
import functools

import jax
import jax.numpy as jnp
from jax import lax
from jax.experimental import pallas as pl
from jax.experimental.pallas import tpu as pltpu
from jax.sharding import PartitionSpec as P

MESH = pl.DeviceIdType.MESH
NS_STEPS = 3
COEFF_A, COEFF_B, COEFF_C = (3.4445, -4.775, 2.0315)
UPDATE_SCALE = 0.5
f32, bf16 = jnp.float32, jnp.bfloat16
NN = (((1,), (0,)), ((), ()))
NT = (((1,), (1,)), ((), ()))


def dot(a, b, dims=NN):
    return lax.dot_general(a, b, dims, preferred_element_type=f32)


def split(a):
    high = a.astype(bf16)
    return high, (a - high.astype(f32)).astype(bf16)


def orthogonalize(grads):
    wide = [g.astype(f32) for g in grads]
    scales = [lax.rsqrt(jnp.sum(g * g) + 1e-06) for g in wide]
    states = None
    for repeat in range(NS_STEPS):
        if repeat == 0:
            highs = grads
            grams = [(s * s) * dot(h, h, NT) for h, s in zip(highs, scales)]
        else:
            highs = [x.astype(bf16) for x in states]
            grams = [dot(h, h, NT) for h in highs]
        lows = [m.astype(bf16) for m in grams]
        squares = [dot(m, m) for m in lows]
        polys = [COEFF_B * m + COEFF_C * s for m, s in zip(grams, squares)]
        if repeat == 0:
            moves = [dot(p.astype(bf16), h) for p, h in zip(polys, highs)]
            states = [s * (COEFF_A * x + m) for s, x, m in zip(scales, wide, moves)]
        elif repeat + 1 < NS_STEPS:
            moves = [dot(p.astype(bf16), h) for p, h in zip(polys, highs)]
            states = [COEFF_A * x + m for x, m in zip(states, moves)]
        else:
            moves = []
            for p, x in zip(polys, states):
                (ph, pl_), (xh, xl) = split(p), split(x)
                moves.append(dot(ph, xh) + (dot(ph, xl) + dot(pl_, xh)))
            states = [COEFF_A * x + m for x, m in zip(states, moves)]
    return states


def kernel(
    groups, rows_y, rows_x,
    q_ref, k_ref, v_ref, r_ref, gi_ref, ui_ref, di_ref,
    oq_ref, rows_ref,
    qbuf, vbuf, rates, ke, kbuf, sbuf, rbuf, gbuf, own, wg, state, wlow, osl, win, oin,
    load, feed_s, feed_r, rs_s, rs_r, ag_s, ag_r, fw_s, fw_r, in_s, in_r, if_s, if_r, w_s, w_r, o_s, o_r,
):
    chips = rows_y * rows_x
    g = lax.axis_index("group")
    tok = lax.axis_index("tok")
    core = lax.rem(tok, 2)
    chip = tok // 2
    py, px = chip // rows_x, lax.rem(chip, rows_x)
    sib = chip * 2 + (1 - core)
    tokens, width = ke.shape[1], ke.shape[2]
    hid = state.shape[1]
    half = hid // 2
    per = width * half // 128 // chips
    share = own.shape[1]

    def ring(d, n):
        return min(d, n - d)

    offsets = [(dy, dx) for dy in range(rows_y) for dx in range(rows_x) if (dy, dx) != (0, 0)]
    offsets.sort(key=lambda o: (-(ring(o[0], rows_y) + ring(o[1], rows_x)), o[1] == 3, o[0] == 3, o[1]))
    count = len(offsets)

    def ahead(n):
        dy, dx = offsets[n]
        return lax.rem(py + dy, rows_y) * rows_x + lax.rem(px + dx, rows_x)

    def behind(n):
        dy, dx = offsets[n]
        return lax.rem(py + (rows_y - dy), rows_y) * rows_x + lax.rem(px + (rows_x - dx), rows_x)

    def copy(src, dst, send, recv, where):
        return pltpu.make_async_remote_copy(
            src_ref=src, dst_ref=dst, send_sem=send, recv_sem=recv, device_id=where, device_id_type=MESH
        )

    loads = [
        pltpu.make_async_copy(v_ref.at[0], vbuf, load.at[0]),
        pltpu.make_async_copy(r_ref, rates, load.at[1]),
        pltpu.make_async_copy(k_ref.at[0], ke.at[0], load.at[2]),
        pltpu.make_async_copy(q_ref.at[0], qbuf, load.at[3]),
    ]
    barrier = pltpu.get_barrier_semaphore()

    def scale_values():
        for n in range(3):
            loads[n].wait()
        rate = jnp.broadcast_to(rates[...].astype(f32), (width, tokens)).T
        ke[1] = (-(rate * vbuf[...].astype(f32))).astype(bf16)

    def query(weights):
        pre = dot(qbuf[...], weights[0], NT)
        up = dot(qbuf[...], weights[1], NT)
        hidden = (pre * (0.5 + 0.5 * jnp.tanh(0.5 * pre)) * up).astype(bf16)
        oq_ref[0] = dot(hidden, weights[2]).astype(bf16)

    @pl.when(g > 0)
    def _():
        for n in range(4):
            loads[n].start()
        scale_values()
        pl.semaphore_wait(barrier, 1)
        feed = copy(ke, kbuf.at[g, core], feed_s, feed_r.at[g, core], (0, tok))
        feed.start()
        loads[3].wait()
        copy(wlow, win, w_s, w_r, (0, tok)).wait_recv()
        query([win[m] for m in range(3)])
        copy(osl, oin, o_s, o_r, (0, tok)).wait_recv()
        rows_ref[...] = oin[...]
        feed.wait_send()

    @pl.when(g == 0)
    def _():
        for z in range(1, groups):
            pl.semaphore_signal(barrier, inc=1, device_id=(z, tok), device_id_type=MESH)
        firsts = [
            pltpu.make_async_copy(ref, own.at[m], load.at[4 + m])
            for m, ref in enumerate((gi_ref, ui_ref, di_ref))
        ]
        for c in firsts:
            c.start()
        for n in range(4):
            loads[n].start()
        for n in range(count):
            pl.semaphore_signal(barrier, inc=1, device_id=(0, ahead(n) * 2 + core), device_id_type=MESH)
        pl.semaphore_signal(barrier, inc=1, device_id=(0, sib), device_id_type=MESH)
        for c in firsts:
            c.wait()
        for w, value in enumerate(split(own[...].reshape(3 * share, hid))):
            wg[tok, w] = value
        pl.semaphore_wait(barrier, count + 1)

        def first_copy(w, n):
            slot = wg.at[tok, w]
            return copy(slot, slot, in_s.at[w, n], in_r.at[w, n], (0, ahead(n) * 2 + core))

        def first_pass(w, n):
            slot = wg.at[tok if n == count else behind(n) * 2 + core, w]
            return copy(slot, slot, if_s.at[w, n], if_r.at[w, n], (0, sib))

        def first_parts(w):
            wide = wg[:, w].astype(f32)
            gate, up, down = (
                wide[:, m * share : (m + 1) * share].reshape(width, hid) for m in range(3)
            )
            return gate.T, up.T, down

        def first_sent(w):
            for n in range(count):
                first_copy(w, n).wait_send()
            for n in range(count + 1):
                first_pass(w, n).wait_send()

        for n in range(count):
            first_copy(0, n).start()
        first_pass(0, count).start()
        scale_values()
        kbuf[0, core] = ke[...]
        feed = copy(ke, kbuf.at[0, core], feed_s, feed_r.at[0, core], (0, sib))
        feed.start()
        loads[3].wait()
        for n in reversed(range(count)):
            first_copy(0, n).wait_recv()
            first_pass(0, n).start()
        for n in reversed(range(count + 1)):
            first_pass(0, n).wait_recv()
        for m, value in enumerate(first_parts(0)):
            state[m] = value
        wlow[...] = state[...].astype(bf16)
        feed.wait_send()

        def pick_outgoing():
            rows = lax.broadcasted_iota(jnp.int32, (16, width), 0)
            lanes = lax.broadcasted_iota(jnp.int32, (16, width), 1)
            for part in range(0, share, 16):
                size = min(16, share - part)
                one = jnp.where(lanes == rows + (tok * share + part), 1.0, 0.0).astype(bf16)
                for m in range(2):
                    full = state[m]
                    high, rest = split(full)
                    mid, low = split(full - high.astype(f32))
                    picked = dot(one, high, NT) + (dot(one, mid, NT) + dot(one, low, NT))
                    osl[m, part : part + size, :] = picked[:size]
            osl[2] = state[2, pl.ds(pl.multiple_of(tok * share, share), share), :]

        def slice_copy(n):
            return copy(
                sbuf.at[ahead(n)], rbuf.at[n], rs_s.at[n], rs_r.at[n], (0, ahead(n) * 2 + core)
            )

        def sum_copy(par, n):
            slot = gbuf.at[par, core, chip]
            return copy(slot, slot, ag_s.at[n], ag_r.at[n], (0, ahead(n) * 2 + core))

        def pass_copy(par, n):
            slot = gbuf.at[par, core, chip if n == count else behind(n)]
            return copy(slot, slot, fw_s.at[n], fw_r.at[par, n], (0, sib))

        def sums_sent(par):
            for n in range(count):
                sum_copy(par, n).wait_send()
            for n in range(count + 1):
                pass_copy(par, n).wait_send()

        def step(i, carry):
            par = lax.rem(i, 2)
            copy(ke, kbuf.at[i, 1 - core], feed_s, feed_r.at[i, 1 - core], (0, sib)).wait_recv()
            keys = kbuf[i, :, 0].reshape(2 * tokens, width)
            errs = kbuf[i, :, 1].reshape(2 * tokens, width)
            mine = pl.ds(pl.multiple_of(core * half, half), half)
            pre = dot(wlow[0, mine, :], keys, NT)
            up = dot(wlow[1, mine, :], keys, NT)
            back = dot(wlow[2, mine, :], errs, NT)
            sig = 0.5 + 0.5 * jnp.tanh(0.5 * pre)
            act = pre * sig
            slope = sig + act * (1.0 - sig)
            act_low = (act * up).astype(bf16)
            gate_diff = (back * up * slope).astype(bf16)
            up_diff = (back * act).astype(bf16)
            partial = (dot(gate_diff, keys), dot(up_diff, keys), dot(act_low, errs))
            for m in range(3):
                low = partial[m].astype(bf16)
                for s in range(width // 128):
                    span = chips * 128 // width
                    sbuf[s * span : (s + 1) * span, m] = low[:, s * 128 : (s + 1) * 128].reshape(
                        span, per, 128
                    )
            for n in range(count):
                slice_copy(n).start()

            weights_out = copy(wlow, win, w_s, w_r, (i, tok))
            slices_out = copy(osl, oin, o_s, o_r, (i - 1, tok))

            @pl.when(i == 0)
            def _():
                for n in range(count):
                    first_copy(1, n).start()
                first_pass(1, count).start()
                query([wlow[m] for m in range(3)])
                first_sent(0)

            @pl.when(i > 0)
            def _():
                weights_out.start()
                pick_outgoing()
                sums_sent(1 - par)

            @pl.when(i == 1)
            def _():
                rows_ref[...] = osl[...]

            @pl.when(i > 1)
            def _():
                slices_out.start()

            for n in reversed(range(count)):
                slice_copy(n).wait_recv()
            total = sbuf[chip].astype(f32)
            for n in range(count):
                total = total + rbuf[n].astype(f32)
            gbuf[par, core, chip] = total.astype(bf16)

            for n in range(count):
                sum_copy(par, n).start()
            pass_copy(par, count).start()
            for n in range(count):
                slice_copy(n).wait_send()
            for n in reversed(range(count)):
                sum_copy(par, n).wait_recv()
                pass_copy(par, n).start()
            for n in reversed(range(count + 1)):
                pass_copy(par, n).wait_recv()

            coming = jnp.minimum(i + 1, groups - 1)
            pass_feed = copy(
                kbuf.at[coming, core], kbuf.at[coming, core], feed_s, feed_r.at[coming, core], (0, sib)
            )

            @pl.when(i < groups - 1)
            def _():
                pass_feed.wait_recv()
                pass_feed.start()

            @pl.when(i == 0)
            def _():
                for n in reversed(range(count)):
                    first_copy(1, n).wait_recv()
                    first_pass(1, n).start()

            grads = []
            for m in range(3):
                sides = []
                for c in range(2):
                    span = chips * 128 // width
                    sides.append(
                        jnp.concatenate(
                            [
                                gbuf[par, c, s * span : (s + 1) * span, m].reshape(half, 128)
                                for s in range(width // 128)
                            ],
                            axis=1,
                        )
                    )
                grads.append(jnp.concatenate(sides, axis=0))
            ortho = orthogonalize(grads)

            @pl.when(i < groups - 1)
            def _():
                pass_feed.wait_send()

            @pl.when(i > 0)
            def _():
                weights_out.wait_send()

            @pl.when(i > 1)
            def _():
                slices_out.wait_send()

            @pl.when(i == 0)
            def _():
                for n in reversed(range(count + 1)):
                    first_pass(1, n).wait_recv()
                for m, value in enumerate(first_parts(1)):
                    state[m] = state[m] + value
                first_sent(1)

            for m in range(3):
                before = state[m]
                stepped = before - UPDATE_SCALE * ortho[m]
                axis = 0 if m == 2 else 1
                target = jnp.sum(before * before, axis=axis, keepdims=True)
                present = jnp.sum(stepped * stepped, axis=axis, keepdims=True)
                after = stepped * (jnp.sqrt(target) * lax.rsqrt(present + 1e-06))
                state[m] = after
                wlow[m] = after.astype(bf16)
            return carry

        lax.fori_loop(0, groups, step, 0)
        pick_outgoing()
        last = copy(osl, oin, o_s, o_r, (groups - 1, tok))
        last.start()
        sums_sent((groups - 1) % 2)
        last.wait_send()


def solution(mesh):
    groups, devices = mesh.shape["group"], mesh.shape["tok"]
    chips = devices // 2
    rows_y = 4 if chips == 16 else 2
    rows_x = chips // rows_y

    def body(*args):
        _, key_rows, _, _, gate_init, _, down_init = args
        tokens, width = key_rows.shape[1:]
        share, hid = gate_init.shape
        share_w = down_init.shape[0]
        per = width * (hid // 2) // 128 // chips
        count = chips - 1
        vmem = pl.BlockSpec(memory_space=pltpu.VMEM)
        dma = pltpu.SemaphoreType.DMA
        outputs, slices = pl.pallas_call(
            functools.partial(kernel, groups, rows_y, rows_x),
            out_shape=(
                jax.ShapeDtypeStruct((1, tokens, width), bf16),
                jax.ShapeDtypeStruct((3, share, hid), f32),
            ),
            in_specs=[pl.BlockSpec(memory_space=pltpu.MemorySpace.HBM)] * 7,
            out_specs=(vmem,) * 2,
            scratch_shapes=[
                pltpu.VMEM((tokens, width), bf16),
                pltpu.VMEM((tokens, width), bf16),
                pltpu.VMEM((1, tokens), bf16),
                pltpu.VMEM((2, tokens, width), bf16),
                pltpu.VMEM((groups, 2, 2, tokens, width), bf16),
                pltpu.VMEM((chips, 3, per, 128), bf16),
                pltpu.VMEM((count, 3, per, 128), bf16),
                pltpu.VMEM((2, 2, chips, 3, per, 128), bf16),
                pltpu.VMEM((3, share, hid), f32),
                pltpu.VMEM((devices, 2, 3 * share, hid), bf16),
                pltpu.VMEM((3, hid, width), f32),
                pltpu.VMEM((3, hid, width), bf16),
                pltpu.VMEM((3, share, hid), f32),
                pltpu.VMEM((3, hid, width), bf16),
                pltpu.VMEM((3, share, hid), f32),
                dma((7,)),
                dma,
                dma((groups, 2)),
                dma((count,)),
                dma((count,)),
                dma((count,)),
                dma((count,)),
                dma((chips,)),
                dma((2, chips)),
                dma((2, count)),
                dma((2, count)),
                dma((2, chips)),
                dma((2, chips)),
                dma,
                dma,
                dma,
                dma,
            ],
            compiler_params=pltpu.CompilerParams(
                collective_id=0, has_side_effects=True, vmem_limit_bytes=48 * 1024 * 1024
            ),
            cost_estimate=pl.CostEstimate(flops=10**10, bytes_accessed=10**7, transcendentals=10**6),
        )(*[pltpu.with_memory_space_constraint(x, pltpu.MemorySpace.HBM) for x in args])
        return outputs, slices[0:1], slices[1:2], slices[2:3]

    rows = P("group", "tok", None)
    return jax.shard_map(
        body,
        mesh=mesh,
        in_specs=(rows, rows, rows, P("group", "tok"), P("tok", None), P("tok", None), P("tok", None)),
        out_specs=(rows, rows, rows, rows),
        check_vma=False,
    )
```
